32 devices in a mesh: layer: 2 (over y), facet: 16 (over z, x, core).
Axes of the slice: x: 2, y: 2, z: 4, core: 2. Of those that a mesh axis runs over, the one named last changes fastest.
Arguments:
- slabs: bfloat16 [2, 2, 64, 49152], P('layer', None, None, 'facet'), may hold values from -6 to 6
- window: float32 [49152], P('facet'), may hold values from 0.5 to 1.5
- density: int32 [2, 64, 8192], P('layer', None, 'facet'), may hold values from 0 to 7
- offsets: int32 [16], replicated, may hold values from 0 to 49151
Outputs:
- image_out: float32 [2, 64, 49152], P(None, 'layer', 'facet')
The draws below stay inside these ranges and needn't reach their ends.
All inputs are finite; a program needn't handle non-finite values.
Results may differ from the reference program's by a relative error of at most 0.0052.
Values may be sent and summed in bfloat16 or wider, within the bound.
A program may use at most 64 MiB of HBM per device.

```python
import math
import jax
import jax.numpy as jnp
from jax import lax

FACET = 3072
CONTRIB = 128
SUB = 512
COLS = 64
LAYERS = 2
FACETS = 16
IMAGE = 49152


def touch_ends(drawn, rng, smallest, largest):
    longest = drawn.shape.index(max(drawn.shape))
    spots = []
    for shift in (0, 1):
        where = [jax.random.randint(jax.random.fold_in(rng, axis), (), 0, length) for axis, length in enumerate(drawn.shape)]
        where[longest] = (where[longest] + shift) % drawn.shape[longest]
        spots.append(tuple(where))
    return drawn.at[spots[0]].set(smallest).at[spots[1]].set(largest)


def levels(stream_key, extent, shards, least, top_value):
    def one(dim, blocks):
        steps = jax.random.uniform(jax.random.fold_in(jax.random.fold_in(stream_key, 6), dim), (blocks,), jnp.float32, least / len(shards), top_value / len(shards))
        return jnp.repeat(jnp.exp(steps), extent[dim] // blocks).reshape((-1,) + (1,) * (len(extent) - dim - 1))

    gain = one(*shards[0])
    for cut in shards[1:]:
        gain = gain * one(*cut)
    return gain


def gaussian(own_key, shape, spread, most, shards=(), held_as=jnp.bfloat16):
    gain = levels(own_key, shape, shards, -0.22, 0.18) if shards else 1.0
    result = jax.random.normal(own_key, shape, jnp.float32) * spread * gain
    return jnp.minimum(jnp.maximum(result, -most), most).astype(held_as)


def setup_inputs(seed: int = 0) -> dict:
    streams_of = jax.random.split(jax.random.key(seed), 5)
    return {
        "slabs": gaussian(streams_of[0], (LAYERS, 2, COLS, IMAGE), 1.0, 6.0, ((0, 2), (3, 16))),
        "window": jnp.clip(0.5 + 1.0 * jax.random.uniform(streams_of[1], (IMAGE,), jnp.float32) ** levels(streams_of[1], (IMAGE,), ((0, 16),), -0.2, 0.2), 0.5, 1.5),
        "density": touch_ends(jax.random.randint(streams_of[2], (LAYERS, COLS, FACETS * SUB), 0, 8), jax.random.fold_in(streams_of[2], 1), 0, 7).astype(jnp.int32),
        "offsets": touch_ends(jax.random.randint(streams_of[3], (FACETS,), 0, IMAGE), jax.random.fold_in(streams_of[3], 1), 0, IMAGE - 1).astype(jnp.int32),
    }


two_pi = 2.0 * math.pi


def mulmod(left_term, right_term, modulus):
    upper_part = right_term // 256
    lower_part = right_term % 256
    return jnp.mod(jnp.mod(left_term * upper_part, modulus) * 256 + left_term * lower_part, modulus)


def encode_table(offset_block, x_start, facet_width, contrib_len, sample_step, image_width):
    frequencies = jnp.mod(offset_block[:, None] + sample_step * jnp.arange(contrib_len, dtype=jnp.int32)[None, :], image_width)
    places = x_start + jnp.arange(facet_width, dtype=jnp.int32)
    phase_turns = mulmod(frequencies[:, :, None], places[None, None, :], image_width)
    phase_angle = phase_turns.astype(jnp.float32) * (-two_pi / image_width)
    return jnp.stack([jnp.cos(phase_angle), jnp.sin(phase_angle)], 1).astype(jnp.bfloat16)


def embed_table(facet_count, facet_width, contrib_len, sub_len, image_width):
    sample_step = sub_len // contrib_len
    centres = jnp.arange(facet_count, dtype=jnp.int32) * facet_width + facet_width // 2
    sample_pos = jnp.arange(contrib_len, dtype=jnp.int32) * sample_step
    cell_ids = jnp.arange(sub_len, dtype=jnp.int32)
    spacing = cell_ids[None, :] - sample_pos[:, None]
    phase_turns = jnp.mod(spacing[None, :, :] * centres[:, None, None], image_width)
    phase_angle = phase_turns.astype(jnp.float32) * (-two_pi / image_width)
    scaled = spacing.astype(jnp.float32) / sample_step
    kernel = 1.0 / (1.0 + scaled * scaled)
    return jnp.stack([jnp.cos(phase_angle) * kernel, jnp.sin(phase_angle) * kernel], 1).astype(jnp.bfloat16)


def reference(slabs, window, density, offsets):
    sample_step = SUB // CONTRIB
    image_width = FACET * FACETS
    blocks = FACETS // 4
    windowed = (slabs.astype(jnp.float32) * window[None, None, None, :]).astype(jnp.bfloat16)
    block_ids = jnp.arange(blocks, dtype=jnp.int32)
    facet_ids = jnp.arange(FACETS, dtype=jnp.int32)

    def encode_facet(facet_id):
        facet_piece = lax.dynamic_slice_in_dim(windowed, facet_id * FACET, FACET, 3).astype(jnp.float32)

        def one_block(block_id):
            phase_table = encode_table(lax.dynamic_slice_in_dim(offsets, block_id * 4, 4, 0), facet_id * FACET, FACET, CONTRIB, sample_step, image_width).astype(jnp.float32)
            raw_prod = jnp.einsum("lpcx,bqjx->lpcbqj", facet_piece, phase_table)
            real_part = raw_prod[:, 0, :, :, 0] - raw_prod[:, 1, :, :, 1]
            imag_part = raw_prod[:, 0, :, :, 1] + raw_prod[:, 1, :, :, 0]
            return jnp.stack([real_part, imag_part], 1)

        pieces = lax.map(one_block, block_ids)
        pieces = jnp.transpose(pieces, (1, 0, 4, 2, 3, 5)).reshape(LAYERS, FACETS, 2, COLS, CONTRIB)
        return (pieces * FACET ** -0.5).astype(jnp.bfloat16)

    encoded = lax.map(encode_facet, facet_ids)
    embed_phase = embed_table(FACETS, FACET, CONTRIB, SUB, image_width).astype(jnp.float32)

    def subgrid_pass(sub_id):
        received = lax.dynamic_index_in_dim(encoded, sub_id, 2, keepdims=False).astype(jnp.float32)
        raw_prod = jnp.einsum("flpcj,fqju->lpcqu", received, embed_phase)
        real_part = raw_prod[:, 0, :, 0] - raw_prod[:, 1, :, 1]
        imag_part = raw_prod[:, 0, :, 1] + raw_prod[:, 1, :, 0]
        counts = lax.dynamic_slice_in_dim(density, sub_id * SUB, SUB, 2)
        weights = jnp.where(counts > 0, 1.0 / jnp.maximum(counts, 1).astype(jnp.float32), jnp.zeros(counts.shape, jnp.float32))
        gridded = (jnp.stack([real_part, imag_part], 1) * weights[:, None] * (2 * FACETS) ** -0.5).astype(jnp.bfloat16)
        raw_back = jnp.einsum("lpcu,fqju->lpcfqj", gridded.astype(jnp.float32), embed_phase)
        real_back = raw_back[:, 0, :, :, 0] + raw_back[:, 1, :, :, 1]
        imag_back = raw_back[:, 1, :, :, 0] - raw_back[:, 0, :, :, 1]
        return (jnp.stack([real_back, imag_back], 1) * 0.5).astype(jnp.bfloat16)

    returned = lax.map(subgrid_pass, facet_ids)

    def adjoint_facet(facet_id):
        row_block = lax.dynamic_index_in_dim(returned, facet_id, 4, keepdims=False)

        def one_block(running, block_id):
            phase_table = encode_table(lax.dynamic_slice_in_dim(offsets, block_id * 4, 4, 0), facet_id * FACET, FACET, CONTRIB, sample_step, image_width).astype(jnp.float32)
            part_rows = lax.dynamic_slice_in_dim(row_block, block_id * 4, 4, 0).astype(jnp.float32)
            raw_prod = jnp.einsum("blpcj,bqjx->lpcqx", part_rows, phase_table)
            real_part = raw_prod[:, 0, :, 0] + raw_prod[:, 1, :, 1]
            imag_part = raw_prod[:, 1, :, 0] - raw_prod[:, 0, :, 1]
            return running + jnp.stack([real_part, imag_part], 1), None

        running, unused = lax.scan(one_block, jnp.zeros((LAYERS, 2, COLS, FACET), jnp.float32), block_ids)
        taper_row = lax.dynamic_slice_in_dim(window, facet_id * FACET, FACET, 0)
        return jnp.sum(running * taper_row * (FACETS * CONTRIB) ** -0.5, axis=0)

    facet_out = lax.map(adjoint_facet, facet_ids)
    return jnp.transpose(facet_out, (1, 2, 0, 3)).reshape(2, COLS, FACETS * FACET)
```

```python
import functools
import math

import jax
import jax.numpy as jnp
from jax import lax
from jax.experimental import pallas as pl
from jax.experimental.pallas import tpu as pltpu
from jax.sharding import PartitionSpec as P

CONTRIB = 128
SUB = 512
GROUP = 4
CHUNK = 512
ROWS = 256
STEP = SUB // CONTRIB
CHUNKS = 2

MESH = pl.DeviceIdType.MESH


def sincos(turns, period):
    quarter = jnp.floor(turns.astype(jnp.float32) * (4.0 / period) + 0.5).astype(jnp.int32)
    rest = 4 * turns - quarter * period
    y = rest.astype(jnp.float32) * (0.5 * math.pi / period)
    z = y * y
    s = y + y * z * (-1.0 / 6 + z * (1.0 / 120 + z * (-1.0 / 5040 + z * (1.0 / 362880))))
    c = 1.0 + z * (-0.5 + z * (1.0 / 24 + z * (-1.0 / 720 + z * (1.0 / 40320))))
    odd = (quarter & 1) == 1
    cos_abs = jnp.where(odd, s, c)
    sin_abs = jnp.where(odd, c, s)
    cos_part = jnp.where(((quarter + 1) & 2) == 2, -cos_abs, cos_abs)
    sin_part = jnp.where((quarter & 2) == 2, -sin_abs, sin_abs)
    return cos_part, sin_part


def remainder(value, period):
    return value - jnp.floor(value.astype(jnp.float32) * (1.0 / period)).astype(jnp.int32) * period


def kernel(
    layers, facets, cols, width, chunks,
    slab_ref, window_ref, density_ref, offset_ref,
    out_ref,
    slab, counts, window_here, offset_here, wind, ca, sa, table, modulated, acc,
    send1, recv1, embed, kr, ki, rr, ri, raw,
    send2, recv2,
    ssem1, rsem1, ssem2, rsem2, csem, local_sem, up_sem, down_sem,
):
    layer = lax.axis_index("layer")
    me = lax.axis_index("facet")
    image = facets * width
    groups = facets // GROUP
    part = cols // layers
    wide = part // chunks
    band = layers * wide
    mine = me // GROUP
    half = mine // (groups // 2)
    half_groups = groups // 2

    def outward(step):
        return jnp.where(
            half == 0,
            lax.rem(half_groups + step, groups),
            lax.rem(half_groups - 1 - step + groups, groups),
        )

    def inward(step):
        return jnp.where(half == 0, step, groups - 1 - step)

    def signal(sem, where):
        pl.semaphore_signal(sem, inc=1, device_id=where, device_id_type=MESH)

    barrier = pltpu.get_barrier_semaphore()
    for l in range(layers):
        there = lax.rem(layer + l, layers)
        for o in range(GROUP):
            if l > 0 or o > 0:
                signal(barrier, (there, mine * GROUP + lax.rem(me + o, GROUP)))

            @pl.when(mine > 0)
            def _():
                signal(barrier, (there, (mine - 1) * GROUP + lax.rem(me + o, GROUP)))

            @pl.when(mine < groups - 1)
            def _():
                signal(barrier, (there, (mine + 1) * GROUP + lax.rem(me + o, GROUP)))

    fetch_offsets = pltpu.make_async_copy(offset_ref, offset_here, local_sem.at[2])
    fetch_offsets.start()
    fetch_window = pltpu.make_async_copy(window_ref, window_here, local_sem.at[1])
    fetch_window.start()
    fetch_slab = pltpu.make_async_copy(slab_ref, slab, local_sem.at[0])
    fetch_slab.start()

    def relay(d, wanted_up, wanted_down):
        has_up = mine + d <= groups - 1
        has_down = mine - d >= 0

        @pl.when(jnp.logical_and(has_up, wanted_up))
        def _():
            pl.semaphore_wait(up_sem.at[d], 1)
            if d + 1 < groups:

                @pl.when(mine > 0)
                def _():
                    signal(up_sem.at[d + 1], (layer, me - GROUP))

        @pl.when(jnp.logical_and(has_down, wanted_down))
        def _():
            pl.semaphore_wait(down_sem.at[d], 1)
            if d + 1 < groups:

                @pl.when(mine < groups - 1)
                def _():
                    signal(down_sem.at[d + 1], (layer, me + GROUP))

    first_up = jnp.where(half == 0, half_groups - mine, 1)
    first_down = jnp.where(half == 1, mine - half_groups + 1, 1)

    def meet_near():
        at_end = jnp.logical_or(mine == 0, mine == groups - 1)

        @pl.when(at_end)
        def _():
            pl.semaphore_wait(barrier, 2 * GROUP * layers - 1)

        @pl.when(jnp.logical_not(at_end))
        def _():
            pl.semaphore_wait(barrier, 3 * GROUP * layers - 1)
            signal(up_sem.at[2], (layer, me - GROUP))
            signal(down_sem.at[2], (layer, me + GROUP))

    def meet_first():
        for d in range(2, groups):
            relay(d, d <= first_up, d <= first_down)

    def meet_far():
        for d in range(2, groups):
            relay(d, d > first_up, d > first_down)

    lane = lax.broadcasted_iota(jnp.int32, (ROWS, CONTRIB), 1) * STEP
    row = lax.broadcasted_iota(jnp.int32, (ROWS, CONTRIB), 0)
    base_c, base_s = sincos(remainder(lane * me, facets) * width + remainder(lane * row, image), image)
    small = lax.broadcasted_iota(jnp.int32, (8, CONTRIB), 1) * STEP
    for k in range(width // ROWS):
        rot_c, rot_s = sincos(remainder(small * (ROWS * k), image), image)
        rot_c = rot_c[0:1]
        rot_s = rot_s[0:1]
        table[k * ROWS:(k + 1) * ROWS, 0:CONTRIB] = (base_c * rot_c - base_s * rot_s).astype(jnp.bfloat16)
        table[k * ROWS:(k + 1) * ROWS, CONTRIB:2 * CONTRIB] = (
            base_c * rot_s + base_s * rot_c
        ).astype(jnp.bfloat16)

    fetch_offsets.wait()
    square = (GROUP * groups, GROUP * groups)
    on_diagonal = lax.broadcasted_iota(jnp.int32, square, 0) == lax.broadcasted_iota(jnp.int32, square, 1)
    offs = jnp.sum(
        jnp.where(on_diagonal, offset_here[...].astype(jnp.float32), 0.0), axis=1, keepdims=True
    ).astype(jnp.int32)
    start = remainder(offs * me, facets) * width
    cell = lax.broadcasted_iota(jnp.int32, (facets, width), 1)
    turns = start + remainder(offs * cell, image)
    cos_a, sin_a = sincos(turns, image)
    ca[...] = cos_a
    sa[...] = sin_a

    fetch_window.wait()
    fetch_slab.wait()
    window = window_here[...]
    for p in range(2):
        whole = (slab[0, p].astype(jnp.float32) * window).astype(jnp.bfloat16).astype(jnp.float32)
        for q in range(chunks):
            for h in range(layers):
                at = h * part + q * wide
                wind[q, p * band + h * wide:p * band + (h + 1) * wide, :] = whole[at:at + wide]

    meet_near()
    for l in range(layers):

        @pl.when(layer == l)
        def _():
            pltpu.make_async_copy(
                density_ref.at[0, l * part:(l + 1) * part], counts.at[l], csem.at[layers]
            ).start()

        @pl.when(layer != l)
        def _():
            pltpu.make_async_remote_copy(
                src_ref=density_ref.at[0, l * part:(l + 1) * part], dst_ref=counts.at[layer],
                send_sem=csem.at[l], recv_sem=csem.at[layers],
                device_id=(l, me), device_id_type=MESH,
            ).start()

    scale1 = width ** -0.5

    def encode(turn, carry):
        q = turn // groups
        step = lax.rem(turn, groups)
        g = outward(step)
        for k in range(width // CHUNK):
            xs = slice(k * CHUNK, (k + 1) * CHUNK)
            for t in range(GROUP):
                s = g * GROUP + t
                c_row = ca[pl.ds(s, 1), xs]
                s_row = sa[pl.ds(s, 1), xs]
                wr = wind[q, 0:band, xs]
                wi = wind[q, band:2 * band, xs]
                lo = t * 2 * band
                modulated[k % 2, lo:lo + band, :] = (wr * c_row + wi * s_row).astype(jnp.bfloat16)
                modulated[k % 2, lo + band:lo + 2 * band, :] = (wi * c_row - wr * s_row).astype(jnp.bfloat16)
            prod = jnp.dot(modulated[k % 2], table[xs, :], preferred_element_type=jnp.float32)
            if k == 0:
                acc[...] = prod
            else:
                acc[...] += prod
        for t in range(GROUP):
            lo = t * 2 * band
            pr = acc[lo:lo + band, :]
            pi = acc[lo + band:lo + 2 * band, :]
            real = (pr[:, :CONTRIB] + pi[:, CONTRIB:]) * scale1
            imag = (pi[:, :CONTRIB] - pr[:, CONTRIB:]) * scale1
            for h in range(layers):
                hs = slice(h * wide, (h + 1) * wide)
                send1[q, g * GROUP + t, h] = jnp.concatenate([real[hs], imag[hs]], axis=0).astype(jnp.bfloat16)

        @pl.when(turn == 0)
        def _():
            meet_first()

        @pl.when(turn == 1)
        def _():
            meet_far()

        for t in range(GROUP):
            s = g * GROUP + t
            for h in range(layers):
                own = jnp.logical_and(s == me, layer == h)

                @pl.when(jnp.logical_not(own))
                def _():
                    pltpu.make_async_remote_copy(
                        src_ref=send1.at[q, s, h], dst_ref=recv1.at[q, me, layer],
                        send_sem=ssem1.at[q, s, h], recv_sem=rsem1.at[q, mine],
                        device_id=(h, s), device_id_type=MESH,
                    ).start()

                @pl.when(own)
                def _():
                    pltpu.make_async_copy(
                        send1.at[q, s, h], recv1.at[q, me, layer], rsem1.at[q, mine]
                    ).start()

        return carry

    lax.fori_loop(0, chunks * groups, encode, 0)

    spacing = lax.broadcasted_iota(jnp.int32, (CONTRIB, SUB), 1) - STEP * lax.broadcasted_iota(
        jnp.int32, (CONTRIB, SUB), 0
    )
    scaled = spacing.astype(jnp.float32) * (1.0 / STEP)
    weight_k = 1.0 / (1.0 + scaled * scaled)
    c0, s0 = sincos(spacing, 2 * facets)
    kr[...] = c0 * weight_k
    ki[...] = s0 * weight_k
    c1, s1 = sincos(spacing, facets)
    rr[...] = c1
    ri[...] = s1

    def make_embed(f, carry):
        r = kr[...]
        i = ki[...]
        lo = pl.multiple_of(f * CONTRIB, CONTRIB)
        embed[pl.ds(lo, CONTRIB), 0:SUB] = r.astype(jnp.bfloat16)
        embed[pl.ds(lo, CONTRIB), SUB:2 * SUB] = (-i).astype(jnp.bfloat16)
        a = rr[...]
        b = ri[...]
        kr[...] = r * a - i * b
        ki[...] = r * b + i * a
        return carry

    lax.fori_loop(0, facets, make_embed, 0)

    pltpu.make_async_copy(counts, counts, csem.at[layers]).wait()
    sub_scale = (2 * facets) ** -0.5
    dims = (((1,), (1,)), ((), ()))

    def middle(q, carry):
        raw[...] = jnp.zeros_like(raw)

        def gather(step, inner):
            g = inward(step)
            piece = recv1.at[q, pl.ds(g * GROUP, GROUP)]
            pltpu.make_async_copy(piece, piece, rsem1.at[q, g]).wait()
            lhs = jnp.concatenate(
                [recv1[q, g * GROUP + t].reshape(2 * band, CONTRIB) for t in range(GROUP)], axis=1
            )
            lo = pl.multiple_of(g * GROUP * CONTRIB, GROUP * CONTRIB)
            raw[...] += jnp.dot(
                lhs, embed[pl.ds(lo, GROUP * CONTRIB), :], preferred_element_type=jnp.float32
            )
            return inner

        lax.fori_loop(0, groups, gather, 0)

        total_r = jnp.zeros((wide, SUB), jnp.float32)
        total_i = jnp.zeros((wide, SUB), jnp.float32)
        for l in range(layers):
            here = counts[l, pl.ds(pl.multiple_of(q * wide, wide), wide), :]
            weights = jnp.where(
                here > 0, 1.0 / jnp.maximum(here, 1).astype(jnp.float32), 0.0
            )
            re = slice(2 * l * wide, (2 * l + 1) * wide)
            im = slice((2 * l + 1) * wide, (2 * l + 2) * wide)
            raw_r = raw[re, 0:SUB] - raw[im, SUB:2 * SUB]
            raw_i = raw[re, SUB:2 * SUB] + raw[im, 0:SUB]
            total_r += (raw_r * weights * sub_scale).astype(jnp.bfloat16).astype(jnp.float32)
            total_i += (raw_i * weights * sub_scale).astype(jnp.bfloat16).astype(jnp.float32)
        gridded = jnp.concatenate([total_r, total_i], axis=0).astype(jnp.bfloat16)

        def scatter(step, inner):
            g = outward(step)
            lo = pl.multiple_of(g * GROUP * CONTRIB, GROUP * CONTRIB)
            er = embed[pl.ds(lo, GROUP * CONTRIB), 0:SUB]
            ei = embed[pl.ds(lo, GROUP * CONTRIB), SUB:2 * SUB]
            pr = lax.dot_general(gridded, er, dims, preferred_element_type=jnp.float32)
            pi = lax.dot_general(gridded, ei, dims, preferred_element_type=jnp.float32)
            real = (pr[0:wide] + pi[wide:2 * wide]) * 0.5
            imag = (pr[wide:2 * wide] - pi[0:wide]) * 0.5
            both = jnp.concatenate([real, imag], axis=0).astype(jnp.bfloat16)
            for t in range(GROUP):
                send2[q, g * GROUP + t] = both[:, t * CONTRIB:(t + 1) * CONTRIB]
            for t in range(GROUP):
                f = g * GROUP + t

                @pl.when(f != me)
                def _():
                    pltpu.make_async_remote_copy(
                        src_ref=send2.at[q, f], dst_ref=recv2.at[q, me],
                        send_sem=ssem2.at[q, f], recv_sem=rsem2.at[q, mine],
                        device_id=(layer, f), device_id_type=MESH,
                    ).start()

                @pl.when(f == me)
                def _():
                    pltpu.make_async_copy(send2.at[q, f], recv2.at[q, me], rsem2.at[q, mine]).start()

            return inner

        lax.fori_loop(0, groups, scatter, 0)
        return carry

    lax.fori_loop(0, chunks, middle, 0)

    out_ref[...] = jnp.zeros_like(out_ref)
    out_scale = (facets * CONTRIB) ** -0.5

    def adjoint(turn, carry):
        q = turn // groups
        step = lax.rem(turn, groups)
        g = inward(step)
        piece = recv2.at[q, pl.ds(g * GROUP, GROUP)]
        pltpu.make_async_copy(piece, piece, rsem2.at[q, g]).wait()
        tops = []
        for t in range(GROUP):
            both = recv2[q, g * GROUP + t].astype(jnp.float32)
            br = both[0:wide]
            bi = both[wide:2 * wide]
            tops.append(jnp.concatenate([br, -bi], axis=1))
            tops.append(jnp.concatenate([bi, br], axis=1))
        lhs = jnp.concatenate(tops, axis=0).astype(jnp.bfloat16)
        rows = pl.ds(pl.multiple_of(q * wide, wide), wide)
        for k in range(width // CHUNK):
            xs = slice(k * CHUNK, (k + 1) * CHUNK)
            prod = lax.dot_general(lhs, table[xs, :], dims, preferred_element_type=jnp.float32)
            out_r = out_ref[0, rows, xs]
            out_i = out_ref[1, rows, xs]
            for t in range(GROUP):
                s = g * GROUP + t
                c_row = ca[pl.ds(s, 1), xs]
                s_row = sa[pl.ds(s, 1), xs]
                gr = prod[(2 * t) * wide:(2 * t + 1) * wide]
                gi = prod[(2 * t + 1) * wide:(2 * t + 2) * wide]
                out_r = out_r + (c_row * gr - s_row * gi)
                out_i = out_i + (c_row * gi + s_row * gr)
            factor = jnp.where(step == groups - 1, window_here[:, xs] * out_scale, 1.0)
            out_ref[0, rows, xs] = out_r * factor
            out_ref[1, rows, xs] = out_i * factor
        return carry

    lax.fori_loop(0, chunks * groups, adjoint, 0)

    def drain(turn, carry):
        q = turn // facets
        s = lax.rem(turn, facets)
        for h in range(layers):

            @pl.when(jnp.logical_not(jnp.logical_and(s == me, layer == h)))
            def _():
                pltpu.make_async_remote_copy(
                    src_ref=send1.at[q, s, h], dst_ref=recv1.at[q, s, h],
                    send_sem=ssem1.at[q, s, h], recv_sem=rsem1.at[q, mine],
                    device_id=(h, s), device_id_type=MESH,
                ).wait_send()

        @pl.when(s != me)
        def _():
            pltpu.make_async_remote_copy(
                src_ref=send2.at[q, s], dst_ref=recv2.at[q, s],
                send_sem=ssem2.at[q, s], recv_sem=rsem2.at[q, mine],
                device_id=(layer, s), device_id_type=MESH,
            ).wait_send()

        return carry

    lax.fori_loop(0, chunks * facets, drain, 0)
    for l in range(layers):

        @pl.when(layer != l)
        def _():
            pltpu.make_async_remote_copy(
                src_ref=density_ref.at[0, l * part:(l + 1) * part], dst_ref=counts.at[l],
                send_sem=csem.at[l], recv_sem=csem.at[layers],
                device_id=(l, me), device_id_type=MESH,
            ).wait_send()


def shards(slabs, window, density, offsets):
    facets = lax.axis_size("facet")
    layers = lax.axis_size("layer")
    cols = slabs.shape[2]
    width = slabs.shape[3]
    part = cols // layers
    chunks = CHUNKS if part % (16 * CHUNKS) == 0 else 1
    wide = part // chunks
    f32, bf16 = jnp.float32, jnp.bfloat16
    summed = pl.pallas_call(
        functools.partial(kernel, layers, facets, cols, width, chunks),
        out_shape=jax.ShapeDtypeStruct((2, part, width), f32),
        in_specs=[pl.BlockSpec(memory_space=pltpu.HBM)] * 4,
        out_specs=pl.BlockSpec(memory_space=pltpu.VMEM),
        scratch_shapes=[
            pltpu.VMEM(slabs.shape, bf16),
            pltpu.VMEM((layers, part, SUB), jnp.int32),
            pltpu.VMEM((1, width), f32),
            pltpu.VMEM((1, facets), jnp.int32),
            pltpu.VMEM((chunks, 2 * layers * wide, width), f32),
            pltpu.VMEM((facets, width), f32),
            pltpu.VMEM((facets, width), f32),
            pltpu.VMEM((width, 2 * CONTRIB), bf16),
            pltpu.VMEM((2, GROUP * 2 * layers * wide, CHUNK), bf16),
            pltpu.VMEM((GROUP * 2 * layers * wide, 2 * CONTRIB), f32),
            pltpu.VMEM((chunks, facets, layers, 2 * wide, CONTRIB), bf16),
            pltpu.VMEM((chunks, facets, layers, 2 * wide, CONTRIB), bf16),
            pltpu.VMEM((facets * CONTRIB, 2 * SUB), bf16),
            pltpu.VMEM((CONTRIB, SUB), f32),
            pltpu.VMEM((CONTRIB, SUB), f32),
            pltpu.VMEM((CONTRIB, SUB), f32),
            pltpu.VMEM((CONTRIB, SUB), f32),
            pltpu.VMEM((2 * layers * wide, 2 * SUB), f32),
            pltpu.VMEM((chunks, facets, 2 * wide, CONTRIB), bf16),
            pltpu.VMEM((chunks, facets, 2 * wide, CONTRIB), bf16),
            pltpu.SemaphoreType.DMA((chunks, facets, layers)),
            pltpu.SemaphoreType.DMA((chunks, facets // GROUP)),
            pltpu.SemaphoreType.DMA((chunks, facets)),
            pltpu.SemaphoreType.DMA((chunks, facets // GROUP)),
            pltpu.SemaphoreType.DMA((layers + 1,)),
            pltpu.SemaphoreType.DMA((3,)),
            pltpu.SemaphoreType.REGULAR((facets // GROUP,)),
            pltpu.SemaphoreType.REGULAR((facets // GROUP,)),
        ],
        compiler_params=pltpu.CompilerParams(
            collective_id=0, has_side_effects=True, vmem_limit_bytes=(14 + facets) * 1024 * 1024
        ),
    )(
        *(
            pltpu.with_memory_space_constraint(x, pltpu.HBM)
            for x in (slabs, window[None, :], density, offsets[None, :])
        )
    )
    return summed


def solution(mesh):
    placed = (P("layer", None, None, "facet"), P("facet"), P("layer", None, "facet"), P())
    return jax.shard_map(
        shards, mesh=mesh, in_specs=placed, out_specs=P(None, "layer", "facet"), check_vma=False
    )
```

```python
import functools
import math

import jax
import jax.numpy as jnp
from jax import lax
from jax.experimental import pallas as pl
from jax.experimental.pallas import tpu as pltpu
from jax.sharding import PartitionSpec as P

CONTRIB = 128
SUB = 512
GROUP = 4
CHUNK = 512
ROWS = 256
STEP = SUB // CONTRIB

MESH = pl.DeviceIdType.MESH

S, X, Y, D = (0, 0), (1, 0), (0, 1), (1, 1)
END_TURNS = (1, 3, 0, 2)
END_PLAN = (
    ((1, S),),
    ((1, X),),
    ((3, S), (0, S), (0, X), (0, Y), (0, D),),
    ((3, X), (3, Y),),
    ((3, D), (1, Y), (1, D), (2, S), (2, X), (2, Y), (2, D),),
)
INNER_TURNS = (2, 3, 0, 1)
INNER_PLAN = (
    ((2, S),),
    ((3, S), (2, X),),
    ((3, X), (3, Y),),
    ((3, D), (0, S), (0, X), (0, Y), (0, D), (2, Y), (2, D), (1, S), (1, X), (1, Y), (1, D),),
    (),
)


def sincos(turns, period):
    quarter = jnp.floor(turns.astype(jnp.float32) * (4.0 / period) + 0.5).astype(jnp.int32)
    rest = 4 * turns - quarter * period
    y = rest.astype(jnp.float32) * (0.5 * math.pi / period)
    z = y * y
    s = y + y * z * (-1.0 / 6 + z * (1.0 / 120 + z * (-1.0 / 5040 + z * (1.0 / 362880))))
    c = 1.0 + z * (-0.5 + z * (1.0 / 24 + z * (-1.0 / 720 + z * (1.0 / 40320))))
    odd = (quarter & 1) == 1
    cos_abs = jnp.where(odd, s, c)
    sin_abs = jnp.where(odd, c, s)
    cos_part = jnp.where(((quarter + 1) & 2) == 2, -cos_abs, cos_abs)
    sin_part = jnp.where((quarter & 2) == 2, -sin_abs, sin_abs)
    return cos_part, sin_part


def remainder(value, period):
    return value - jnp.floor(value.astype(jnp.float32) * (1.0 / period)).astype(jnp.int32) * period


def kernel(
    layers, facets, cols, width,
    slab_ref, window_ref, density_ref, offset_ref,
    out_ref,
    slab, counts, window_here, offset_here, wind, ca, sa, table, modulated, acc,
    send1, recv1, embed, kr, ki, rr, ri, raw,
    send2, recv2,
    ssem1, rsem1, ssem2, rsem2, csem, local_sem, reach_sem,
):
    layer = lax.axis_index("layer")
    me = lax.axis_index("facet")
    image = facets * width
    groups = facets // GROUP
    part = cols // layers
    band = layers * part
    mine = me // GROUP
    half = mine // (groups // 2)
    half_groups = groups // 2

    def ranked(step, end, inner):
        mirrored = jnp.where(half == 0, mine, groups - 1 - mine)
        g = jnp.where(mirrored == 0, end[0], inner[0])
        for i in range(1, groups):
            g = jnp.where(step == i, jnp.where(mirrored == 0, end[i], inner[i]), g)
        return jnp.where(half == 0, g, groups - 1 - g)

    def encode_order(step):
        if groups == 4:
            return ranked(step, END_TURNS, INNER_TURNS)
        return outward(step)

    def gather_order(step):
        if groups == 4:
            return ranked(step, (0, 1, 2, 3), (1, 0, 3, 2))
        return inward(step)

    def scatter_order(step):
        if groups == 4:
            return ranked(step, (3, 1, 2, 0), (3, 2, 0, 1))
        return outward(step)

    def adjoint_order(step):
        if groups == 4:
            return ranked(step, (0, 3, 1, 2), (0, 3, 1, 2))
        return inward(step)

    def outward(step):
        return jnp.where(
            half == 0,
            lax.rem(half_groups + step, groups),
            lax.rem(half_groups - 1 - step + groups, groups),
        )

    def inward(step):
        return jnp.where(half == 0, step, groups - 1 - step)

    def signal(sem, where):
        pl.semaphore_signal(sem, inc=1, device_id=where, device_id_type=MESH)

    near = [(layer, me ^ 2)] + [(lax.rem(layer + l, layers), me) for l in range(1, layers)]
    has_up = mine < groups - 1
    has_down = mine > 0

    barrier = pltpu.get_barrier_semaphore()
    signal(barrier, (layer, me ^ 1))
    for core in range(2):
        for there, f in near:
            signal(barrier, (there, f ^ core))

        @pl.when(has_up)
        def _():
            signal(barrier, (layer, (me + GROUP) ^ core))

        @pl.when(has_down)
        def _():
            signal(barrier, (layer, (me - GROUP) ^ core))

    fetch_offsets = pltpu.make_async_copy(offset_ref, offset_here, local_sem.at[2])
    fetch_offsets.start()
    fetch_window = pltpu.make_async_copy(window_ref, window_here, local_sem.at[1])
    fetch_window.start()
    fetch_slab = pltpu.make_async_copy(slab_ref, slab, local_sem.at[0])
    fetch_slab.start()

    def tell(reach):
        for where in near:
            signal(reach_sem.at[reach], where)

        @pl.when(has_up)
        def _():
            signal(reach_sem.at[reach], (layer, me + GROUP))

        @pl.when(has_down)
        def _():
            signal(reach_sem.at[reach], (layer, me - GROUP))

    def meet(reach):
        @pl.when(jnp.logical_and(has_up, has_down))
        def _():
            pl.semaphore_wait(reach_sem.at[reach], len(near) + 2)

        @pl.when(jnp.logical_not(jnp.logical_and(has_up, has_down)))
        def _():
            pl.semaphore_wait(reach_sem.at[reach], len(near) + 1)

    lane = lax.broadcasted_iota(jnp.int32, (ROWS, CONTRIB), 1) * STEP
    row = lax.broadcasted_iota(jnp.int32, (ROWS, CONTRIB), 0)
    base_c, base_s = sincos(remainder(lane * me, facets) * width + remainder(lane * row, image), image)
    small = lax.broadcasted_iota(jnp.int32, (8, CONTRIB), 1) * STEP
    for k in range(width // ROWS):
        rot_c, rot_s = sincos(remainder(small * (ROWS * k), image), image)
        rot_c = rot_c[0:1]
        rot_s = rot_s[0:1]
        table[k * ROWS:(k + 1) * ROWS, 0:CONTRIB] = (base_c * rot_c - base_s * rot_s).astype(jnp.bfloat16)
        table[k * ROWS:(k + 1) * ROWS, CONTRIB:2 * CONTRIB] = (
            base_c * rot_s + base_s * rot_c
        ).astype(jnp.bfloat16)

    fetch_offsets.wait()
    square = (GROUP * groups, GROUP * groups)
    on_diagonal = lax.broadcasted_iota(jnp.int32, square, 0) == lax.broadcasted_iota(jnp.int32, square, 1)
    offs = jnp.sum(
        jnp.where(on_diagonal, offset_here[...].astype(jnp.float32), 0.0), axis=1, keepdims=True
    ).astype(jnp.int32)
    start = remainder(offs * me, facets) * width
    cell = lax.broadcasted_iota(jnp.int32, (facets, width), 1)
    turns = start + remainder(offs * cell, image)
    cos_a, sin_a = sincos(turns, image)
    ca[...] = cos_a
    sa[...] = sin_a

    fetch_window.wait()
    fetch_slab.wait()
    window = window_here[...]
    for p in range(2):
        whole = (slab[0, p].astype(jnp.float32) * window).astype(jnp.bfloat16).astype(jnp.float32)
        wind[p * band:(p + 1) * band, :] = whole

    scale1 = width ** -0.5

    def deliver(h, s):
        pltpu.make_async_remote_copy(
            src_ref=send1.at[s * layers + h], dst_ref=recv1.at[me, layer],
            send_sem=ssem1, recv_sem=rsem1.at[mine],
            device_id=(h, s), device_id_type=MESH,
        ).start()

    def planned(turn):
        outer = jnp.logical_or(mine == 0, mine == groups - 1)
        for i in range(groups + 1):
            for at_end, plan in ((True, END_PLAN[i]), (False, INNER_PLAN[i])):
                if not plan:
                    continue

                @pl.when(jnp.logical_and(turn == i, outer if at_end else jnp.logical_not(outer)))
                def _():
                    for g, (dx, dl) in plan:
                        there = jnp.where(half == 0, g, groups - 1 - g)
                        straight = there * GROUP + lax.rem(me, GROUP)
                        home = g == (0 if at_end else 1) and not dx and not dl
                        for core in range(2):
                            if home and core == 0:
                                pltpu.make_async_copy(
                                    send1.at[me * layers + layer], recv1.at[me, layer], rsem1.at[mine]
                                ).start()
                            else:
                                deliver(layer ^ dl, straight ^ (2 * dx + core))

    def dispatch(turn):
        if groups == 4 and layers == 2:
            planned(turn)
            return

        def slot(a, carry):
            g = encode_order(a)
            ahead = jnp.abs(g - mine)
            straight = g * GROUP + lax.rem(me, GROUP)
            for off in range(3):
                reach = ahead + off
                late = jnp.logical_and(a < turn, reach == turn + 1)
                fresh = jnp.logical_and(a == turn, reach <= turn + 1)

                @pl.when(jnp.logical_or(late, fresh))
                def _():
                    if off == 0:
                        deliver(layer, straight ^ 1)

                        @pl.when(g != mine)
                        def _():
                            deliver(layer, straight)

                        @pl.when(g == mine)
                        def _():
                            pltpu.make_async_copy(
                                send1.at[me * layers + layer], recv1.at[me, layer], rsem1.at[mine]
                            ).start()

                    for core in range(2):
                        if off == 1:
                            deliver(layer, straight ^ (2 + core))
                        if off > 0:
                            for l in range(1, layers):
                                deliver(lax.rem(layer + l, layers), straight ^ (2 * off - 2 + core))

            return carry

        lax.fori_loop(0, groups, slot, 0)

    def encode(turn, carry):
        step = turn
        g = encode_order(step)
        for k in range(width // CHUNK):
            xs = slice(k * CHUNK, (k + 1) * CHUNK)
            for t in range(GROUP):
                s = g * GROUP + t
                c_row = ca[pl.ds(s, 1), xs]
                s_row = sa[pl.ds(s, 1), xs]
                wr = wind[0:band, xs]
                wi = wind[band:2 * band, xs]
                lo = t * 2 * band
                modulated[k % 2, lo:lo + band, :] = (wr * c_row + wi * s_row).astype(jnp.bfloat16)
                modulated[k % 2, lo + band:lo + 2 * band, :] = (wi * c_row - wr * s_row).astype(jnp.bfloat16)
            prod = jnp.dot(modulated[k % 2], table[xs, :], preferred_element_type=jnp.float32)
            if k == 0:
                acc[...] = prod
            else:
                acc[...] += prod
        for t in range(GROUP):
            lo = t * 2 * band
            pr = acc[lo:lo + band, :]
            pi = acc[lo + band:lo + 2 * band, :]
            real = (pr[:, :CONTRIB] + pi[:, CONTRIB:]) * scale1
            imag = (pi[:, :CONTRIB] - pr[:, CONTRIB:]) * scale1
            for h in range(layers):
                hs = slice(h * part, (h + 1) * part)
                send1[(g * GROUP + t) * layers + h] = jnp.concatenate([real[hs], imag[hs]], axis=0).astype(jnp.bfloat16)

        @pl.when(turn == 0)
        def _():
            both = jnp.logical_and(has_up, has_down)

            @pl.when(both)
            def _():
                pl.semaphore_wait(barrier, 1 + 2 * (len(near) + 2))

            @pl.when(jnp.logical_not(both))
            def _():
                pl.semaphore_wait(barrier, 1 + 2 * (len(near) + 1))

            tell(2)

        @pl.when(turn > 0)
        def _():
            meet(turn + 1)
            tell(turn + 2)

        dispatch(turn)

        @pl.when(turn == 0)
        def _():
            for l in range(layers):

                @pl.when(layer == l)
                def _():
                    pltpu.make_async_copy(
                        density_ref.at[0, l * part:(l + 1) * part], counts.at[l], csem.at[1]
                    ).start()

                @pl.when(layer != l)
                def _():
                    pltpu.make_async_remote_copy(
                        src_ref=density_ref.at[0, l * part:(l + 1) * part], dst_ref=counts.at[layer],
                        send_sem=csem.at[0], recv_sem=csem.at[1],
                        device_id=(l, me), device_id_type=MESH,
                    ).start()

        return carry

    lax.fori_loop(0, groups, encode, 0)
    meet(groups + 1)
    dispatch(groups)

    spacing = lax.broadcasted_iota(jnp.int32, (CONTRIB, SUB), 1) - STEP * lax.broadcasted_iota(
        jnp.int32, (CONTRIB, SUB), 0
    )
    scaled = spacing.astype(jnp.float32) * (1.0 / STEP)
    weight_k = 1.0 / (1.0 + scaled * scaled)
    c0, s0 = sincos(spacing, 2 * facets)
    kr[...] = c0 * weight_k
    ki[...] = s0 * weight_k
    c1, s1 = sincos(spacing, facets)
    rr[...] = c1
    ri[...] = s1

    def make_embed(f, carry):
        r = kr[...]
        i = ki[...]
        lo = pl.multiple_of(f * CONTRIB, CONTRIB)
        embed[pl.ds(lo, CONTRIB), 0:SUB] = r.astype(jnp.bfloat16)
        embed[pl.ds(lo, CONTRIB), SUB:2 * SUB] = (-i).astype(jnp.bfloat16)
        a = rr[...]
        b = ri[...]
        kr[...] = r * a - i * b
        ki[...] = r * b + i * a
        return carry

    lax.fori_loop(0, facets, make_embed, 0)

    pltpu.make_async_copy(counts, counts, csem.at[1]).wait()
    sub_scale = (2 * facets) ** -0.5
    dims = (((1,), (1,)), ((), ()))

    raw[...] = jnp.zeros_like(raw)

    def gather(step, inner):
        g = gather_order(step)
        piece = recv1.at[pl.ds(g * GROUP, GROUP)]
        pltpu.make_async_copy(piece, piece, rsem1.at[g]).wait()
        lhs = jnp.concatenate(
            [recv1[g * GROUP + t].reshape(2 * band, CONTRIB) for t in range(GROUP)], axis=1
        )
        lo = pl.multiple_of(g * GROUP * CONTRIB, GROUP * CONTRIB)
        raw[...] += jnp.dot(
            lhs, embed[pl.ds(lo, GROUP * CONTRIB), :], preferred_element_type=jnp.float32
        )
        return inner

    lax.fori_loop(0, groups, gather, 0)

    total_r = jnp.zeros((part, SUB), jnp.float32)
    total_i = jnp.zeros((part, SUB), jnp.float32)
    for l in range(layers):
        here = counts[l]
        weights = jnp.where(
            here > 0, 1.0 / jnp.maximum(here, 1).astype(jnp.float32), 0.0
        )
        re = slice(2 * l * part, (2 * l + 1) * part)
        im = slice((2 * l + 1) * part, (2 * l + 2) * part)
        raw_r = raw[re, 0:SUB] - raw[im, SUB:2 * SUB]
        raw_i = raw[re, SUB:2 * SUB] + raw[im, 0:SUB]
        total_r += (raw_r * weights * sub_scale).astype(jnp.bfloat16).astype(jnp.float32)
        total_i += (raw_i * weights * sub_scale).astype(jnp.bfloat16).astype(jnp.float32)
    gridded = jnp.concatenate([total_r, total_i], axis=0).astype(jnp.bfloat16)

    def scatter(step, inner):
        g = scatter_order(step)
        lo = pl.multiple_of(g * GROUP * CONTRIB, GROUP * CONTRIB)
        er = embed[pl.ds(lo, GROUP * CONTRIB), 0:SUB]
        ei = embed[pl.ds(lo, GROUP * CONTRIB), SUB:2 * SUB]
        pr = lax.dot_general(gridded, er, dims, preferred_element_type=jnp.float32)
        pi = lax.dot_general(gridded, ei, dims, preferred_element_type=jnp.float32)
        real = (pr[0:part] + pi[part:2 * part]) * 0.5
        imag = (pr[part:2 * part] - pi[0:part]) * 0.5
        both = jnp.concatenate([real, imag], axis=0).astype(jnp.bfloat16)
        for t in range(GROUP):
            send2[g * GROUP + t] = both[:, t * CONTRIB:(t + 1) * CONTRIB]
        for t in range(GROUP):
            f = g * GROUP + t

            @pl.when(f != me)
            def _():
                pltpu.make_async_remote_copy(
                    src_ref=send2.at[f], dst_ref=recv2.at[me],
                    send_sem=ssem2, recv_sem=rsem2.at[mine],
                    device_id=(layer, f), device_id_type=MESH,
                ).start()

            @pl.when(f == me)
            def _():
                pltpu.make_async_copy(send2.at[f], recv2.at[me], rsem2.at[mine]).start()

        return inner

    lax.fori_loop(0, groups, scatter, 0)

    out_ref[...] = jnp.zeros_like(out_ref)
    out_scale = (facets * CONTRIB) ** -0.5

    def adjoint(turn, carry):
        step = turn
        g = adjoint_order(step)
        piece = recv2.at[pl.ds(g * GROUP, GROUP)]
        pltpu.make_async_copy(piece, piece, rsem2.at[g]).wait()
        tops = []
        for t in range(GROUP):
            both = recv2[g * GROUP + t].astype(jnp.float32)
            br = both[0:part]
            bi = both[part:2 * part]
            tops.append(jnp.concatenate([br, -bi], axis=1))
            tops.append(jnp.concatenate([bi, br], axis=1))
        lhs = jnp.concatenate(tops, axis=0).astype(jnp.bfloat16)
        for k in range(width // CHUNK):
            xs = slice(k * CHUNK, (k + 1) * CHUNK)
            prod = lax.dot_general(lhs, table[xs, :], dims, preferred_element_type=jnp.float32)
            out_r = out_ref[0, :, xs]
            out_i = out_ref[1, :, xs]
            for t in range(GROUP):
                s = g * GROUP + t
                c_row = ca[pl.ds(s, 1), xs]
                s_row = sa[pl.ds(s, 1), xs]
                gr = prod[(2 * t) * part:(2 * t + 1) * part]
                gi = prod[(2 * t + 1) * part:(2 * t + 2) * part]
                out_r = out_r + (c_row * gr - s_row * gi)
                out_i = out_i + (c_row * gi + s_row * gr)
            factor = jnp.where(step == groups - 1, window_here[:, xs] * out_scale, 1.0)
            out_ref[0, :, xs] = out_r * factor
            out_ref[1, :, xs] = out_i * factor
        return carry

    lax.fori_loop(0, groups, adjoint, 0)

    for ref, sem in (
        (send1.at[pl.ds(0, facets * layers - 1)], ssem1),
        (send2.at[pl.ds(0, facets - 1)], ssem2),
        (counts.at[pl.ds(0, layers - 1)], csem.at[0]),
    ):
        pltpu.make_async_copy(ref, ref, sem).wait()


def shards(slabs, window, density, offsets):
    facets = lax.axis_size("facet")
    layers = lax.axis_size("layer")
    cols = slabs.shape[2]
    width = slabs.shape[3]
    part = cols // layers
    f32, bf16 = jnp.float32, jnp.bfloat16
    summed = pl.pallas_call(
        functools.partial(kernel, layers, facets, cols, width),
        out_shape=jax.ShapeDtypeStruct((2, part, width), f32),
        in_specs=[pl.BlockSpec(memory_space=pltpu.HBM)] * 4,
        out_specs=pl.BlockSpec(memory_space=pltpu.VMEM),
        scratch_shapes=[
            pltpu.VMEM(slabs.shape, bf16),
            pltpu.VMEM((layers, part, SUB), jnp.int32),
            pltpu.VMEM((1, width), f32),
            pltpu.VMEM((1, facets), jnp.int32),
            pltpu.VMEM((2 * layers * part, width), f32),
            pltpu.VMEM((facets, width), f32),
            pltpu.VMEM((facets, width), f32),
            pltpu.VMEM((width, 2 * CONTRIB), bf16),
            pltpu.VMEM((2, GROUP * 2 * layers * part, CHUNK), bf16),
            pltpu.VMEM((GROUP * 2 * layers * part, 2 * CONTRIB), f32),
            pltpu.VMEM((facets * layers, 2 * part, CONTRIB), bf16),
            pltpu.VMEM((facets, layers, 2 * part, CONTRIB), bf16),
            pltpu.VMEM((facets * CONTRIB, 2 * SUB), bf16),
            pltpu.VMEM((CONTRIB, SUB), f32),
            pltpu.VMEM((CONTRIB, SUB), f32),
            pltpu.VMEM((CONTRIB, SUB), f32),
            pltpu.VMEM((CONTRIB, SUB), f32),
            pltpu.VMEM((2 * layers * part, 2 * SUB), f32),
            pltpu.VMEM((facets, 2 * part, CONTRIB), bf16),
            pltpu.VMEM((facets, 2 * part, CONTRIB), bf16),
            pltpu.SemaphoreType.DMA,
            pltpu.SemaphoreType.DMA((facets // GROUP,)),
            pltpu.SemaphoreType.DMA,
            pltpu.SemaphoreType.DMA((facets // GROUP,)),
            pltpu.SemaphoreType.DMA((2,)),
            pltpu.SemaphoreType.DMA((3,)),
            pltpu.SemaphoreType.REGULAR((facets // GROUP + 2,)),
        ],
        compiler_params=pltpu.CompilerParams(
            collective_id=0, has_side_effects=True, vmem_limit_bytes=(14 + facets) * 1024 * 1024
        ),
    )(
        *(
            pltpu.with_memory_space_constraint(x, pltpu.HBM)
            for x in (slabs, window[None, :], density, offsets[None, :])
        )
    )
    return summed


def solution(mesh):
    placed = (P("layer", None, None, "facet"), P("facet"), P("layer", None, "facet"), P())
    return jax.shard_map(
        shards, mesh=mesh, in_specs=placed, out_specs=P(None, "layer", "facet"), check_vma=False
    )
```

```python
import functools
import math

import jax
import jax.numpy as jnp
from jax import lax
from jax.experimental import pallas as pl
from jax.experimental.pallas import tpu as pltpu
from jax.sharding import PartitionSpec as P

CONTRIB = 128
SUB = 512
GROUP = 4
CHUNK = 512
ROWS = 256
TILES = 8
STEP = SUB // CONTRIB

MESH = pl.DeviceIdType.MESH

S, X, Y, D = (0, 0), (1, 0), (0, 1), (1, 1)
END_TURNS = (1, 3, 0, 2)
END_PLAN = (
    ((1, S),),
    ((1, X),),
    ((3, S), (0, S), (0, X), (0, Y), (0, D),),
    ((3, X), (3, Y),),
    ((3, D), (1, Y), (1, D), (2, S), (2, X), (2, Y), (2, D),),
)
INNER_TURNS = (2, 3, 0, 1)
INNER_PLAN = (
    ((2, S),),
    ((3, S), (2, X),),
    ((3, X), (3, Y),),
    ((3, D), (0, S), (0, X), (0, Y), (0, D), (2, Y), (2, D), (1, S), (1, X), (1, Y), (1, D),),
    (),
)


def sincos(turns, period):
    quarter = jnp.floor(turns.astype(jnp.float32) * (4.0 / period) + 0.5).astype(jnp.int32)
    rest = 4 * turns - quarter * period
    y = rest.astype(jnp.float32) * (0.5 * math.pi / period)
    z = y * y
    s = y + y * z * (-1.0 / 6 + z * (1.0 / 120 + z * (-1.0 / 5040 + z * (1.0 / 362880))))
    c = 1.0 + z * (-0.5 + z * (1.0 / 24 + z * (-1.0 / 720 + z * (1.0 / 40320))))
    odd = (quarter & 1) == 1
    cos_abs = jnp.where(odd, s, c)
    sin_abs = jnp.where(odd, c, s)
    cos_part = jnp.where(((quarter + 1) & 2) == 2, -cos_abs, cos_abs)
    sin_part = jnp.where((quarter & 2) == 2, -sin_abs, sin_abs)
    return cos_part, sin_part


def remainder(value, period):
    return value - jnp.floor(value.astype(jnp.float32) * (1.0 / period)).astype(jnp.int32) * period


def kernel(
    layers, facets, cols, width,
    slab_ref, window_ref, density_ref, offset_ref,
    out_ref,
    slab, counts, window_here, offset_here, wind, ca, sa, table, modulated, acc,
    send1, recv1, embed, kr, ki, rr, ri, raw,
    send2, recv2, offs_wide, fine, phase_c, phase_s, turned, total,
    ssem1, rsem1, ssem2, rsem2, csem, local_sem, reach_sem,
):
    layer = lax.axis_index("layer")
    me = lax.axis_index("facet")
    image = facets * width
    groups = facets // GROUP
    part = cols // layers
    band = layers * part
    mine = me // GROUP
    half = mine // (groups // 2)
    half_groups = groups // 2

    def ranked(step, end, inner):
        mirrored = jnp.where(half == 0, mine, groups - 1 - mine)
        g = jnp.where(mirrored == 0, end[0], inner[0])
        for i in range(1, groups):
            g = jnp.where(step == i, jnp.where(mirrored == 0, end[i], inner[i]), g)
        return jnp.where(half == 0, g, groups - 1 - g)

    def encode_order(step):
        if groups == 4:
            return ranked(step, END_TURNS, INNER_TURNS)
        return outward(step)

    def gather_order(step):
        if groups == 4:
            return ranked(step, (0, 1, 2, 3), (1, 0, 3, 2))
        return inward(step)

    def scatter_order(step):
        if groups == 4:
            return ranked(step, (3, 0, 1, 2), (0, 1, 3, 2))
        return outward(step)

    def adjoint_order(step):
        if groups == 4:
            return ranked(step, (0, 3, 2, 1), (1, 0, 3, 2))
        return inward(step)

    def outward(step):
        return jnp.where(
            half == 0,
            lax.rem(half_groups + step, groups),
            lax.rem(half_groups - 1 - step + groups, groups),
        )

    def inward(step):
        return jnp.where(half == 0, step, groups - 1 - step)

    def signal(sem, where):
        pl.semaphore_signal(sem, inc=1, device_id=where, device_id_type=MESH)

    near = [(layer, me ^ 2)] + [(lax.rem(layer + l, layers), me) for l in range(1, layers)]
    has_up = mine < groups - 1
    has_down = mine > 0

    barrier = pltpu.get_barrier_semaphore()
    signal(barrier, (layer, me ^ 1))
    for core in range(2):
        for there, f in near:
            signal(barrier, (there, f ^ core))

        @pl.when(has_up)
        def _():
            signal(barrier, (layer, (me + GROUP) ^ core))

        @pl.when(has_down)
        def _():
            signal(barrier, (layer, (me - GROUP) ^ core))

    fetch_offsets = pltpu.make_async_copy(offset_ref, offset_here, local_sem.at[2])
    fetch_offsets.start()
    fetch_window = pltpu.make_async_copy(window_ref, window_here, local_sem.at[1])
    fetch_window.start()
    fetch_slab = pltpu.make_async_copy(slab_ref, slab, local_sem.at[0])
    fetch_slab.start()

    def tell(reach):
        for where in near:
            signal(reach_sem.at[reach], where)

        @pl.when(has_up)
        def _():
            signal(reach_sem.at[reach], (layer, me + GROUP))

        @pl.when(has_down)
        def _():
            signal(reach_sem.at[reach], (layer, me - GROUP))

    def meet(reach):
        @pl.when(jnp.logical_and(has_up, has_down))
        def _():
            pl.semaphore_wait(reach_sem.at[reach], len(near) + 2)

        @pl.when(jnp.logical_not(jnp.logical_and(has_up, has_down)))
        def _():
            pl.semaphore_wait(reach_sem.at[reach], len(near) + 1)

    lane = lax.broadcasted_iota(jnp.int32, (ROWS, CONTRIB), 1) * STEP
    row = lax.broadcasted_iota(jnp.int32, (ROWS, CONTRIB), 0)
    base_c, base_s = sincos(remainder(lane * me, facets) * width + remainder(lane * row, image), image)
    small = lax.broadcasted_iota(jnp.int32, (8, CONTRIB), 1) * STEP
    for k in range(width // ROWS):
        rot_c, rot_s = sincos(remainder(small * (ROWS * k), image), image)
        rot_c = rot_c[0:1]
        rot_s = rot_s[0:1]
        table[k * ROWS:(k + 1) * ROWS, 0:CONTRIB] = (base_c * rot_c - base_s * rot_s).astype(jnp.bfloat16)
        table[k * ROWS:(k + 1) * ROWS, CONTRIB:2 * CONTRIB] = (
            base_c * rot_s + base_s * rot_c
        ).astype(jnp.bfloat16)

    fetch_offsets.wait()
    square = (GROUP * groups, GROUP * groups)
    on_diagonal = lax.broadcasted_iota(jnp.int32, square, 0) == lax.broadcasted_iota(jnp.int32, square, 1)
    offs = jnp.sum(
        jnp.where(on_diagonal, offset_here[...].astype(jnp.float32), 0.0), axis=1, keepdims=True
    ).astype(jnp.int32)
    offs_wide[...] = jnp.broadcast_to(offs, offs_wide.shape)
    start = remainder(offs * me, facets) * width
    cell = lax.broadcasted_iota(jnp.int32, (facets, width), 1)
    turns = start + remainder(offs * cell, image)
    cos_a, sin_a = sincos(turns, image)
    ca[...] = cos_a
    sa[...] = sin_a

    fetch_window.wait()
    fetch_slab.wait()
    window = window_here[...]
    for p in range(2):
        whole = (slab[0, p].astype(jnp.float32) * window).astype(jnp.bfloat16).astype(jnp.float32)
        wind[p * band:(p + 1) * band, :] = whole

    scale1 = width ** -0.5

    def deliver(h, s):
        pltpu.make_async_remote_copy(
            src_ref=send1.at[s * layers + h], dst_ref=recv1.at[me, layer],
            send_sem=ssem1, recv_sem=rsem1.at[mine],
            device_id=(h, s), device_id_type=MESH,
        ).start()

    def planned(turn):
        outer = jnp.logical_or(mine == 0, mine == groups - 1)
        for i in range(groups + 1):
            for at_end, plan in ((True, END_PLAN[i]), (False, INNER_PLAN[i])):
                if not plan:
                    continue

                @pl.when(jnp.logical_and(turn == i, outer if at_end else jnp.logical_not(outer)))
                def _():
                    for g, (dx, dl) in plan:
                        there = jnp.where(half == 0, g, groups - 1 - g)
                        straight = there * GROUP + lax.rem(me, GROUP)
                        home = g == (0 if at_end else 1) and not dx and not dl
                        for core in range(2):
                            if home and core == 0:
                                pltpu.make_async_copy(
                                    send1.at[me * layers + layer], recv1.at[me, layer], rsem1.at[mine]
                                ).start()
                            else:
                                deliver(layer ^ dl, straight ^ (2 * dx + core))

    def dispatch(turn):
        if groups == 4 and layers == 2:
            planned(turn)
            return

        def slot(a, carry):
            g = encode_order(a)
            ahead = jnp.abs(g - mine)
            straight = g * GROUP + lax.rem(me, GROUP)
            for off in range(3):
                reach = ahead + off
                late = jnp.logical_and(a < turn, reach == turn + 1)
                fresh = jnp.logical_and(a == turn, reach <= turn + 1)

                @pl.when(jnp.logical_or(late, fresh))
                def _():
                    if off == 0:
                        deliver(layer, straight ^ 1)

                        @pl.when(g != mine)
                        def _():
                            deliver(layer, straight)

                        @pl.when(g == mine)
                        def _():
                            pltpu.make_async_copy(
                                send1.at[me * layers + layer], recv1.at[me, layer], rsem1.at[mine]
                            ).start()

                    for core in range(2):
                        if off == 1:
                            deliver(layer, straight ^ (2 + core))
                        if off > 0:
                            for l in range(1, layers):
                                deliver(lax.rem(layer + l, layers), straight ^ (2 * off - 2 + core))

            return carry

        lax.fori_loop(0, groups, slot, 0)

    def encode(turn, carry):
        step = turn
        g = encode_order(step)
        for k in range(width // CHUNK):
            xs = slice(k * CHUNK, (k + 1) * CHUNK)
            for t in range(GROUP):
                s = g * GROUP + t
                c_row = ca[pl.ds(s, 1), xs]
                s_row = sa[pl.ds(s, 1), xs]
                wr = wind[0:band, xs]
                wi = wind[band:2 * band, xs]
                lo = t * 2 * band
                modulated[k % 2, lo:lo + band, :] = (wr * c_row + wi * s_row).astype(jnp.bfloat16)
                modulated[k % 2, lo + band:lo + 2 * band, :] = (wi * c_row - wr * s_row).astype(jnp.bfloat16)
            prod = jnp.dot(modulated[k % 2], table[xs, :], preferred_element_type=jnp.float32)
            if k == 0:
                acc[...] = prod
            else:
                acc[...] += prod
        for t in range(GROUP):
            lo = t * 2 * band
            pr = acc[lo:lo + band, :]
            pi = acc[lo + band:lo + 2 * band, :]
            real = (pr[:, :CONTRIB] + pi[:, CONTRIB:]) * scale1
            imag = (pi[:, :CONTRIB] - pr[:, CONTRIB:]) * scale1
            for h in range(layers):
                hs = slice(h * part, (h + 1) * part)
                send1[(g * GROUP + t) * layers + h] = jnp.concatenate([real[hs], imag[hs]], axis=0).astype(jnp.bfloat16)

        @pl.when(turn == 0)
        def _():
            both = jnp.logical_and(has_up, has_down)

            @pl.when(both)
            def _():
                pl.semaphore_wait(barrier, 1 + 2 * (len(near) + 2))

            @pl.when(jnp.logical_not(both))
            def _():
                pl.semaphore_wait(barrier, 1 + 2 * (len(near) + 1))

            tell(2)

        @pl.when(turn > 0)
        def _():
            meet(turn + 1)
            tell(turn + 2)

        dispatch(turn)

        @pl.when(turn == 0)
        def _():
            for l in range(layers):

                @pl.when(layer == l)
                def _():
                    pltpu.make_async_copy(
                        density_ref.at[0, l * part:(l + 1) * part], counts.at[l], csem.at[1]
                    ).start()

                @pl.when(layer != l)
                def _():
                    pltpu.make_async_remote_copy(
                        src_ref=density_ref.at[0, l * part:(l + 1) * part], dst_ref=counts.at[layer],
                        send_sem=csem.at[0], recv_sem=csem.at[1],
                        device_id=(l, me), device_id_type=MESH,
                    ).start()

        return carry

    lax.fori_loop(0, groups, encode, 0)
    meet(groups + 1)
    dispatch(groups)

    spacing = lax.broadcasted_iota(jnp.int32, (CONTRIB, SUB), 1) - STEP * lax.broadcasted_iota(
        jnp.int32, (CONTRIB, SUB), 0
    )
    scaled = spacing.astype(jnp.float32) * (1.0 / STEP)
    weight_k = 1.0 / (1.0 + scaled * scaled)
    c0, s0 = sincos(spacing, 2 * facets)
    kr[...] = c0 * weight_k
    ki[...] = s0 * weight_k
    c1, s1 = sincos(spacing, facets)
    rr[...] = c1
    ri[...] = s1

    def make_embed(f, carry):
        r = kr[...]
        i = ki[...]
        lo = pl.multiple_of(f * CONTRIB, CONTRIB)
        embed[pl.ds(lo, CONTRIB), 0:SUB] = r.astype(jnp.bfloat16)
        embed[pl.ds(lo, CONTRIB), SUB:2 * SUB] = (-i).astype(jnp.bfloat16)
        a = rr[...]
        b = ri[...]
        kr[...] = r * a - i * b
        ki[...] = r * b + i * a
        return carry

    lax.fori_loop(0, facets, make_embed, 0)

    tiles = width // CONTRIB
    square = (CONTRIB, CONTRIB)
    lane_here = lax.broadcasted_iota(jnp.int32, square, 1)
    fine_c, fine_s = sincos(
        remainder(STEP * lax.broadcasted_iota(jnp.int32, square, 0) * lane_here, image), image
    )
    kr[:, 0:CONTRIB] = fine_c
    ki[:, 0:CONTRIB] = fine_s
    coarse = CONTRIB * lax.broadcasted_iota(jnp.int32, (tiles, CONTRIB), 0)
    steps = STEP * lax.broadcasted_iota(jnp.int32, (tiles, CONTRIB), 1)

    def make_phases(f, carry):
        off = offs_wide[pl.ds(f, 1), :]
        c, i = sincos(remainder(off * lane_here[0:1], image), image)
        fc = kr[:, 0:CONTRIB] * c - ki[:, 0:CONTRIB] * i
        fs = kr[:, 0:CONTRIB] * i + ki[:, 0:CONTRIB] * c
        lo = pl.multiple_of(f * 2 * CONTRIB, 2 * CONTRIB)
        fine[pl.ds(lo, CONTRIB), 0:CONTRIB] = fc.astype(jnp.bfloat16)
        fine[pl.ds(lo, CONTRIB), CONTRIB:2 * CONTRIB] = fs.astype(jnp.bfloat16)
        fine[pl.ds(lo + CONTRIB, CONTRIB), 0:CONTRIB] = (-fs).astype(jnp.bfloat16)
        fine[pl.ds(lo + CONTRIB, CONTRIB), CONTRIB:2 * CONTRIB] = fc.astype(jnp.bfloat16)
        frequency = off + steps
        pc, ps = sincos(
            remainder(frequency * me, facets) * width + remainder(frequency * coarse, image), image
        )
        phase_c[f] = pc
        phase_s[f] = ps
        return carry

    lax.fori_loop(0, facets, make_phases, 0)
    total[...] = jnp.zeros_like(total)

    pltpu.make_async_copy(counts, counts, csem.at[1]).wait()
    sub_scale = (2 * facets) ** -0.5
    dims = (((1,), (1,)), ((), ()))

    raw[...] = jnp.zeros_like(raw)

    def gather(step, inner):
        g = gather_order(step)
        piece = recv1.at[pl.ds(g * GROUP, GROUP)]
        pltpu.make_async_copy(piece, piece, rsem1.at[g]).wait()
        lhs = jnp.concatenate(
            [recv1[g * GROUP + t].reshape(2 * band, CONTRIB) for t in range(GROUP)], axis=1
        )
        lo = pl.multiple_of(g * GROUP * CONTRIB, GROUP * CONTRIB)
        raw[...] += jnp.dot(
            lhs, embed[pl.ds(lo, GROUP * CONTRIB), :], preferred_element_type=jnp.float32
        )
        return inner

    lax.fori_loop(0, groups, gather, 0)

    total_r = jnp.zeros((part, SUB), jnp.float32)
    total_i = jnp.zeros((part, SUB), jnp.float32)
    for l in range(layers):
        here = counts[l]
        weights = jnp.where(
            here > 0, 1.0 / jnp.maximum(here, 1).astype(jnp.float32), 0.0
        )
        re = slice(2 * l * part, (2 * l + 1) * part)
        im = slice((2 * l + 1) * part, (2 * l + 2) * part)
        raw_r = raw[re, 0:SUB] - raw[im, SUB:2 * SUB]
        raw_i = raw[re, SUB:2 * SUB] + raw[im, 0:SUB]
        total_r += (raw_r * weights * sub_scale).astype(jnp.bfloat16).astype(jnp.float32)
        total_i += (raw_i * weights * sub_scale).astype(jnp.bfloat16).astype(jnp.float32)
    gridded = jnp.concatenate(
        [
            jnp.concatenate([total_r, total_i], axis=1),
            jnp.concatenate([total_i, -total_r], axis=1),
        ],
        axis=0,
    ).astype(jnp.bfloat16)

    def scatter(step, inner):
        g = scatter_order(step)
        lo = pl.multiple_of(g * GROUP * CONTRIB, GROUP * CONTRIB)
        back = lax.dot_general(
            gridded, embed[pl.ds(lo, GROUP * CONTRIB), :], dims, preferred_element_type=jnp.float32
        )
        both = (back * 0.5).astype(jnp.bfloat16)
        for t in range(GROUP):
            send2[g * GROUP + t] = both[:, t * CONTRIB:(t + 1) * CONTRIB]
        for t in range(GROUP):
            f = g * GROUP + t

            @pl.when(f != me)
            def _():
                pltpu.make_async_remote_copy(
                    src_ref=send2.at[f], dst_ref=recv2.at[me],
                    send_sem=ssem2, recv_sem=rsem2.at[mine],
                    device_id=(layer, f), device_id_type=MESH,
                ).start()

            @pl.when(f == me)
            def _():
                pltpu.make_async_copy(send2.at[f], recv2.at[me], rsem2.at[mine]).start()

        return inner

    lax.fori_loop(0, groups, scatter, 0)

    out_scale = (facets * CONTRIB) ** -0.5

    def adjoint(step, last):
        g = adjoint_order(step)
        piece = recv2.at[pl.ds(g * GROUP, GROUP)]
        pltpu.make_async_copy(piece, piece, rsem2.at[g]).wait()
        lo = pl.multiple_of(g * GROUP * 2 * CONTRIB, GROUP * 2 * CONTRIB)
        for k in range(tiles // TILES):
            lhs = []
            for t in range(GROUP):
                both = recv2[g * GROUP + t].astype(jnp.float32)
                br = both[0:part]
                bi = both[part:2 * part]
                turned_r = []
                turned_i = []
                for i in range(TILES):
                    pc = phase_c[g * GROUP + t, k * TILES + i:k * TILES + i + 1, :]
                    ps = phase_s[g * GROUP + t, k * TILES + i:k * TILES + i + 1, :]
                    turned_r.append(br * pc - bi * ps)
                    turned_i.append(br * ps + bi * pc)
                lhs.append(jnp.concatenate(turned_r, axis=0).astype(jnp.bfloat16))
                lhs.append(jnp.concatenate(turned_i, axis=0).astype(jnp.bfloat16))
            rows = slice(k * TILES * part, (k + 1) * TILES * part)
            new = total[rows, :] + jnp.dot(
                jnp.concatenate(lhs, axis=1), fine[pl.ds(lo, GROUP * 2 * CONTRIB), :], preferred_element_type=jnp.float32
            )
            if not last:
                total[rows, :] = new
                continue
            for i in range(TILES):
                xs = slice((k * TILES + i) * CONTRIB, (k * TILES + i + 1) * CONTRIB)
                factor = window_here[:, xs] * out_scale
                out_ref[0, :, xs] = new[i * part:(i + 1) * part, 0:CONTRIB] * factor
                out_ref[1, :, xs] = new[i * part:(i + 1) * part, CONTRIB:2 * CONTRIB] * factor

    def early(step, carry):
        adjoint(step, False)
        return carry

    lax.fori_loop(0, groups - 1, early, 0)
    adjoint(groups - 1, True)

    for ref, sem in (
        (send1.at[pl.ds(0, facets * layers - 1)], ssem1),
        (send2.at[pl.ds(0, facets - 1)], ssem2),
        (counts.at[pl.ds(0, layers - 1)], csem.at[0]),
    ):
        pltpu.make_async_copy(ref, ref, sem).wait()


def shards(slabs, window, density, offsets):
    facets = lax.axis_size("facet")
    layers = lax.axis_size("layer")
    cols = slabs.shape[2]
    width = slabs.shape[3]
    part = cols // layers
    f32, bf16 = jnp.float32, jnp.bfloat16
    summed = pl.pallas_call(
        functools.partial(kernel, layers, facets, cols, width),
        out_shape=jax.ShapeDtypeStruct((2, part, width), f32),
        in_specs=[pl.BlockSpec(memory_space=pltpu.HBM)] * 4,
        out_specs=pl.BlockSpec(memory_space=pltpu.VMEM),
        scratch_shapes=[
            pltpu.VMEM(slabs.shape, bf16),
            pltpu.VMEM((layers, part, SUB), jnp.int32),
            pltpu.VMEM((1, width), f32),
            pltpu.VMEM((1, facets), jnp.int32),
            pltpu.VMEM((2 * layers * part, width), f32),
            pltpu.VMEM((facets, width), f32),
            pltpu.VMEM((facets, width), f32),
            pltpu.VMEM((width, 2 * CONTRIB), bf16),
            pltpu.VMEM((2, GROUP * 2 * layers * part, CHUNK), bf16),
            pltpu.VMEM((GROUP * 2 * layers * part, 2 * CONTRIB), f32),
            pltpu.VMEM((facets * layers, 2 * part, CONTRIB), bf16),
            pltpu.VMEM((facets, layers, 2 * part, CONTRIB), bf16),
            pltpu.VMEM((facets * CONTRIB, 2 * SUB), bf16),
            pltpu.VMEM((CONTRIB, SUB), f32),
            pltpu.VMEM((CONTRIB, SUB), f32),
            pltpu.VMEM((CONTRIB, SUB), f32),
            pltpu.VMEM((CONTRIB, SUB), f32),
            pltpu.VMEM((2 * layers * part, 2 * SUB), f32),
            pltpu.VMEM((facets, 2 * part, CONTRIB), bf16),
            pltpu.VMEM((facets, 2 * part, CONTRIB), bf16),
            pltpu.VMEM((facets, CONTRIB), jnp.int32),
            pltpu.VMEM((facets * 2 * CONTRIB, 2 * CONTRIB), bf16),
            pltpu.VMEM((facets, width // CONTRIB, CONTRIB), f32),
            pltpu.VMEM((facets, width // CONTRIB, CONTRIB), f32),
            pltpu.VMEM((2, TILES * part, GROUP * 2 * CONTRIB), bf16),
            pltpu.VMEM((width // CONTRIB * part, 2 * CONTRIB), f32),
            pltpu.SemaphoreType.DMA,
            pltpu.SemaphoreType.DMA((facets // GROUP,)),
            pltpu.SemaphoreType.DMA,
            pltpu.SemaphoreType.DMA((facets // GROUP,)),
            pltpu.SemaphoreType.DMA((2,)),
            pltpu.SemaphoreType.DMA((3,)),
            pltpu.SemaphoreType.REGULAR((facets // GROUP + 2,)),
        ],
        compiler_params=pltpu.CompilerParams(
            collective_id=0, has_side_effects=True, vmem_limit_bytes=(14 + facets) * 1024 * 1024
        ),
    )(
        *(
            pltpu.with_memory_space_constraint(x, pltpu.HBM)
            for x in (slabs, window[None, :], density, offsets[None, :])
        )
    )
    return summed


def solution(mesh):
    placed = (P("layer", None, None, "facet"), P("facet"), P("layer", None, "facet"), P())
    return jax.shard_map(
        shards, mesh=mesh, in_specs=placed, out_specs=P(None, "layer", "facet"), check_vma=False
    )
```

```python
import functools
import math

import jax
import jax.numpy as jnp
from jax import lax
from jax.experimental import pallas as pl
from jax.experimental.pallas import tpu as pltpu
from jax.sharding import PartitionSpec as P

CONTRIB = 128
SUB = 512
GROUP = 4
CHUNK = 512
ROWS = 256
TILES = 8
PAIR = GROUP // 2
STEP = SUB // CONTRIB

MESH = pl.DeviceIdType.MESH

S, X, Y, D = (0, 0), (1, 0), (0, 1), (1, 1)
END_TURNS = (1, 3, 0, 2)
END_PLAN = (
    ((1, S),),
    ((1, X),),
    ((3, S), (0, S), (0, X), (0, Y), (0, D),),
    ((3, X), (3, Y),),
    ((3, D), (1, Y), (1, D), (2, S), (2, X), (2, Y), (2, D),),
)
INNER_TURNS = (2, 3, 0, 1)
INNER_PLAN = (
    ((2, S),),
    ((3, S), (2, X),),
    ((3, X), (3, Y),),
    ((3, D), (0, S), (0, X), (0, Y), (0, D), (2, Y), (2, D), (1, S), (1, X), (1, Y), (1, D),),
    (),
)


def sincos(turns, period):
    quarter = jnp.floor(turns.astype(jnp.float32) * (4.0 / period) + 0.5).astype(jnp.int32)
    rest = 4 * turns - quarter * period
    y = rest.astype(jnp.float32) * (0.5 * math.pi / period)
    z = y * y
    s = y + y * z * (-1.0 / 6 + z * (1.0 / 120 + z * (-1.0 / 5040 + z * (1.0 / 362880))))
    c = 1.0 + z * (-0.5 + z * (1.0 / 24 + z * (-1.0 / 720 + z * (1.0 / 40320))))
    odd = (quarter & 1) == 1
    cos_abs = jnp.where(odd, s, c)
    sin_abs = jnp.where(odd, c, s)
    cos_part = jnp.where(((quarter + 1) & 2) == 2, -cos_abs, cos_abs)
    sin_part = jnp.where((quarter & 2) == 2, -sin_abs, sin_abs)
    return cos_part, sin_part


def remainder(value, period):
    return value - jnp.floor(value.astype(jnp.float32) * (1.0 / period)).astype(jnp.int32) * period


def kernel(
    layers, facets, cols, width,
    slab_ref, window_ref, density_ref, offset_ref,
    out_ref,
    slab, counts, window_here, offset_here, wind, ca, sa, table, modulated, acc,
    send1, recv1, embed, kr, ki, rr, ri, raw,
    send2, recv2, offs_wide, fine, phase_c, phase_s, turned, total, weighting,
    ssem1, rsem1, ssem2, rsem2, csem, local_sem, reach_sem,
):
    layer = lax.axis_index("layer")
    me = lax.axis_index("facet")
    image = facets * width
    groups = facets // GROUP
    part = cols // layers
    band = layers * part
    mine = me // GROUP
    half = mine // (groups // 2)
    half_groups = groups // 2

    def ranked(step, end, inner):
        mirrored = jnp.where(half == 0, mine, groups - 1 - mine)
        g = jnp.where(mirrored == 0, end[0], inner[0])
        for i in range(1, groups):
            g = jnp.where(step == i, jnp.where(mirrored == 0, end[i], inner[i]), g)
        return jnp.where(half == 0, g, groups - 1 - g)

    def encode_order(step):
        if groups == 4:
            return ranked(step, END_TURNS, INNER_TURNS)
        return outward(step)

    def gather_order(step):
        if groups == 4:
            return ranked(step, (0, 1, 2, 3), (1, 0, 3, 2))
        return inward(step)

    def scatter_order(step):
        if groups == 4:
            return ranked(step, (3, 0, 1, 2), (0, 1, 3, 2))
        return outward(step)

    def adjoint_order(step):
        if groups == 4:
            return ranked(step, (0, 3, 2, 1), (1, 0, 3, 2))
        return inward(step)

    def outward(step):
        return jnp.where(
            half == 0,
            lax.rem(half_groups + step, groups),
            lax.rem(half_groups - 1 - step + groups, groups),
        )

    def inward(step):
        return jnp.where(half == 0, step, groups - 1 - step)

    def signal(sem, where):
        pl.semaphore_signal(sem, inc=1, device_id=where, device_id_type=MESH)

    near = [(layer, me ^ 2)] + [(lax.rem(layer + l, layers), me) for l in range(1, layers)]
    has_up = mine < groups - 1
    has_down = mine > 0

    barrier = pltpu.get_barrier_semaphore()
    signal(barrier, (layer, me ^ 1))
    for core in range(2):
        for there, f in near:
            signal(barrier, (there, f ^ core))

        @pl.when(has_up)
        def _():
            signal(barrier, (layer, (me + GROUP) ^ core))

        @pl.when(has_down)
        def _():
            signal(barrier, (layer, (me - GROUP) ^ core))

    fetch_offsets = pltpu.make_async_copy(offset_ref, offset_here, local_sem.at[2])
    fetch_offsets.start()
    fetch_window = pltpu.make_async_copy(window_ref, window_here, local_sem.at[1])
    fetch_window.start()
    fetch_slab = pltpu.make_async_copy(slab_ref, slab, local_sem.at[0])
    fetch_slab.start()

    def tell(reach):
        for where in near:
            signal(reach_sem.at[reach], where)

        @pl.when(has_up)
        def _():
            signal(reach_sem.at[reach], (layer, me + GROUP))

        @pl.when(has_down)
        def _():
            signal(reach_sem.at[reach], (layer, me - GROUP))

    def meet(reach):
        @pl.when(jnp.logical_and(has_up, has_down))
        def _():
            pl.semaphore_wait(reach_sem.at[reach], len(near) + 2)

        @pl.when(jnp.logical_not(jnp.logical_and(has_up, has_down)))
        def _():
            pl.semaphore_wait(reach_sem.at[reach], len(near) + 1)

    def spread_rows(count, stride):
        lane = lax.broadcasted_iota(jnp.int32, (count, CONTRIB), 1) * STEP
        row = lax.broadcasted_iota(jnp.int32, (count, CONTRIB), 0) * stride
        return lane, remainder(lane * row, image)

    lane, turns = spread_rows(8, 1)
    low_c, low_s = sincos(remainder(lane * me, facets) * width + turns, image)
    mid_c, mid_s = sincos(spread_rows(ROWS // 8, 8)[1], image)
    high_c, high_s = sincos(spread_rows(-(-width // ROWS // 8) * 8, ROWS)[1], image)
    base_c = jnp.concatenate(
        [low_c * mid_c[i:i + 1] - low_s * mid_s[i:i + 1] for i in range(ROWS // 8)], axis=0
    )
    base_s = jnp.concatenate(
        [low_c * mid_s[i:i + 1] + low_s * mid_c[i:i + 1] for i in range(ROWS // 8)], axis=0
    )
    for k in range(width // ROWS):
        rot_c = high_c[k:k + 1]
        rot_s = high_s[k:k + 1]
        table[k * ROWS:(k + 1) * ROWS, 0:CONTRIB] = (base_c * rot_c - base_s * rot_s).astype(jnp.bfloat16)
        table[k * ROWS:(k + 1) * ROWS, CONTRIB:2 * CONTRIB] = (
            base_c * rot_s + base_s * rot_c
        ).astype(jnp.bfloat16)

    fetch_offsets.wait()
    square = (GROUP * groups, GROUP * groups)
    on_diagonal = lax.broadcasted_iota(jnp.int32, square, 0) == lax.broadcasted_iota(jnp.int32, square, 1)
    offs = jnp.sum(
        jnp.where(on_diagonal, offset_here[...].astype(jnp.float32), 0.0), axis=1, keepdims=True
    ).astype(jnp.int32)
    offs_wide[...] = jnp.broadcast_to(offs, offs_wide.shape)
    cell = lax.broadcasted_iota(jnp.int32, (facets, CONTRIB), 1)
    tile = jnp.minimum(cell, width // CONTRIB - 1) * CONTRIB
    within_c, within_s = sincos(remainder(offs * cell, image), image)
    tile_c, tile_s = sincos(
        remainder(offs * me, facets) * width + remainder(offs * tile, image), image
    )
    for k in range(width // CONTRIB):
        at_c = tile_c[:, k:k + 1]
        at_s = tile_s[:, k:k + 1]
        xs = slice(k * CONTRIB, (k + 1) * CONTRIB)
        ca[:, xs] = within_c * at_c - within_s * at_s
        sa[:, xs] = within_c * at_s + within_s * at_c

    fetch_window.wait()
    fetch_slab.wait()
    window = window_here[...]
    for p in range(2):
        whole = (slab[0, p].astype(jnp.float32) * window).astype(jnp.bfloat16).astype(jnp.float32)
        wind[p * band:(p + 1) * band, :] = whole

    scale1 = width ** -0.5

    def deliver(h, s):
        pltpu.make_async_remote_copy(
            src_ref=send1.at[s * layers + h], dst_ref=recv1.at[me, layer],
            send_sem=ssem1, recv_sem=rsem1.at[mine],
            device_id=(h, s), device_id_type=MESH,
        ).start()

    def planned(turn):
        outer = jnp.logical_or(mine == 0, mine == groups - 1)
        for i in range(groups + 1):
            for at_end, plan in ((True, END_PLAN[i]), (False, INNER_PLAN[i])):
                if not plan:
                    continue

                @pl.when(jnp.logical_and(turn == i, outer if at_end else jnp.logical_not(outer)))
                def _():
                    for g, (dx, dl) in plan:
                        there = jnp.where(half == 0, g, groups - 1 - g)
                        straight = there * GROUP + lax.rem(me, GROUP)
                        home = g == (0 if at_end else 1) and not dx and not dl
                        for core in range(2):
                            if home and core == 0:
                                pltpu.make_async_copy(
                                    send1.at[me * layers + layer], recv1.at[me, layer], rsem1.at[mine]
                                ).start()
                            else:
                                deliver(layer ^ dl, straight ^ (2 * dx + core))

    def dispatch(turn):
        if groups == 4 and layers == 2:
            planned(turn)
            return

        def slot(a, carry):
            g = encode_order(a)
            ahead = jnp.abs(g - mine)
            straight = g * GROUP + lax.rem(me, GROUP)
            for off in range(3):
                reach = ahead + off
                late = jnp.logical_and(a < turn, reach == turn + 1)
                fresh = jnp.logical_and(a == turn, reach <= turn + 1)

                @pl.when(jnp.logical_or(late, fresh))
                def _():
                    if off == 0:
                        deliver(layer, straight ^ 1)

                        @pl.when(g != mine)
                        def _():
                            deliver(layer, straight)

                        @pl.when(g == mine)
                        def _():
                            pltpu.make_async_copy(
                                send1.at[me * layers + layer], recv1.at[me, layer], rsem1.at[mine]
                            ).start()

                    for core in range(2):
                        if off == 1:
                            deliver(layer, straight ^ (2 + core))
                        if off > 0:
                            for l in range(1, layers):
                                deliver(lax.rem(layer + l, layers), straight ^ (2 * off - 2 + core))

            return carry

        lax.fori_loop(0, groups, slot, 0)

    def encode(turn, carry):
        step = turn
        g = encode_order(step)
        for k in range(width // CHUNK):
            xs = slice(k * CHUNK, (k + 1) * CHUNK)
            for t in range(GROUP):
                s = g * GROUP + t
                c_row = ca[pl.ds(s, 1), xs]
                s_row = sa[pl.ds(s, 1), xs]
                wr = wind[0:band, xs]
                wi = wind[band:2 * band, xs]
                lo = t * 2 * band
                modulated[k % 2, lo:lo + band, :] = (wr * c_row + wi * s_row).astype(jnp.bfloat16)
                modulated[k % 2, lo + band:lo + 2 * band, :] = (wi * c_row - wr * s_row).astype(jnp.bfloat16)
            prod = jnp.dot(modulated[k % 2], table[xs, :], preferred_element_type=jnp.float32)
            if k == 0:
                acc[...] = prod
            else:
                acc[...] += prod
        for t in range(GROUP):
            lo = t * 2 * band
            pr = acc[lo:lo + band, :]
            pi = acc[lo + band:lo + 2 * band, :]
            real = (pr[:, :CONTRIB] + pi[:, CONTRIB:]) * scale1
            imag = (pi[:, :CONTRIB] - pr[:, CONTRIB:]) * scale1
            for h in range(layers):
                hs = slice(h * part, (h + 1) * part)
                send1[(g * GROUP + t) * layers + h] = jnp.concatenate([real[hs], imag[hs]], axis=0).astype(jnp.bfloat16)

        @pl.when(turn == 0)
        def _():
            both = jnp.logical_and(has_up, has_down)

            @pl.when(both)
            def _():
                pl.semaphore_wait(barrier, 1 + 2 * (len(near) + 2))

            @pl.when(jnp.logical_not(both))
            def _():
                pl.semaphore_wait(barrier, 1 + 2 * (len(near) + 1))

            tell(2)

        @pl.when(turn > 0)
        def _():
            meet(turn + 1)
            tell(turn + 2)

        dispatch(turn)

        @pl.when(turn == 0)
        def _():
            for l in range(layers):

                @pl.when(layer == l)
                def _():
                    pltpu.make_async_copy(
                        density_ref.at[0, l * part:(l + 1) * part], counts.at[l], csem.at[1]
                    ).start()

                @pl.when(layer != l)
                def _():
                    pltpu.make_async_remote_copy(
                        src_ref=density_ref.at[0, l * part:(l + 1) * part], dst_ref=counts.at[layer],
                        send_sem=csem.at[0], recv_sem=csem.at[1],
                        device_id=(l, me), device_id_type=MESH,
                    ).start()

        return carry

    lax.fori_loop(0, groups, encode, 0)
    meet(groups + 1)
    dispatch(groups)

    spacing = lax.broadcasted_iota(jnp.int32, (CONTRIB, SUB), 1) - STEP * lax.broadcasted_iota(
        jnp.int32, (CONTRIB, SUB), 0
    )
    scaled = spacing.astype(jnp.float32) * (1.0 / STEP)
    weight_k = 1.0 / (1.0 + scaled * scaled)
    c0, s0 = sincos(spacing, 2 * facets)
    kr[...] = c0 * weight_k
    ki[...] = s0 * weight_k
    c1, s1 = sincos(spacing, facets)
    rr[...] = c1
    ri[...] = s1

    def make_embed(f, carry):
        r = kr[...]
        i = ki[...]
        lo = pl.multiple_of(f * CONTRIB, CONTRIB)
        embed[pl.ds(lo, CONTRIB), 0:SUB] = r.astype(jnp.bfloat16)
        embed[pl.ds(lo, CONTRIB), SUB:2 * SUB] = (-i).astype(jnp.bfloat16)
        a = rr[...]
        b = ri[...]
        kr[...] = r * a - i * b
        ki[...] = r * b + i * a
        return carry

    lax.fori_loop(0, facets, make_embed, 0)

    tiles = width // CONTRIB
    square = (CONTRIB, CONTRIB)
    lane_here = lax.broadcasted_iota(jnp.int32, square, 1)
    fine_c, fine_s = sincos(
        remainder(STEP * lax.broadcasted_iota(jnp.int32, square, 0) * lane_here, image), image
    )
    kr[:, 0:CONTRIB] = fine_c
    ki[:, 0:CONTRIB] = fine_s
    coarse = CONTRIB * lax.broadcasted_iota(jnp.int32, (tiles, CONTRIB), 0)
    steps = STEP * lax.broadcasted_iota(jnp.int32, (tiles, CONTRIB), 1)

    def make_phases(f, carry):
        off = offs_wide[pl.ds(f, 1), :]
        c, i = sincos(remainder(off * lane_here[0:1], image), image)
        fc = kr[:, 0:CONTRIB] * c - ki[:, 0:CONTRIB] * i
        fs = kr[:, 0:CONTRIB] * i + ki[:, 0:CONTRIB] * c
        lo = pl.multiple_of(f * 2 * CONTRIB, 2 * CONTRIB)
        fine[pl.ds(lo, CONTRIB), 0:CONTRIB] = fc.astype(jnp.bfloat16)
        fine[pl.ds(lo, CONTRIB), CONTRIB:2 * CONTRIB] = fs.astype(jnp.bfloat16)
        fine[pl.ds(lo + CONTRIB, CONTRIB), 0:CONTRIB] = (-fs).astype(jnp.bfloat16)
        fine[pl.ds(lo + CONTRIB, CONTRIB), CONTRIB:2 * CONTRIB] = fc.astype(jnp.bfloat16)
        frequency = off + steps
        pc, ps = sincos(
            remainder(frequency * me, facets) * width + remainder(frequency * coarse, image), image
        )
        phase_c[f] = pc
        phase_s[f] = ps
        return carry

    lax.fori_loop(0, facets, make_phases, 0)
    total[...] = jnp.zeros_like(total)

    pltpu.make_async_copy(counts, counts, csem.at[1]).wait()
    sub_scale = (2 * facets) ** -0.5
    dims = (((1,), (1,)), ((), ()))

    for l in range(layers):
        here = counts[l]
        weighting[l] = jnp.where(
            here > 0, 1.0 / jnp.maximum(here, 1).astype(jnp.float32), 0.0
        ) * sub_scale
    raw[...] = jnp.zeros_like(raw)

    def gather(step, inner):
        g = gather_order(step)
        piece = recv1.at[pl.ds(g * GROUP, GROUP)]
        pltpu.make_async_copy(piece, piece, rsem1.at[g]).wait()
        lhs = jnp.concatenate(
            [recv1[g * GROUP + t].reshape(2 * band, CONTRIB) for t in range(GROUP)], axis=1
        )
        lo = pl.multiple_of(g * GROUP * CONTRIB, GROUP * CONTRIB)
        raw[...] += jnp.dot(
            lhs, embed[pl.ds(lo, GROUP * CONTRIB), :], preferred_element_type=jnp.float32
        )
        return inner

    lax.fori_loop(0, groups, gather, 0)

    total_r = jnp.zeros((part, SUB), jnp.float32)
    total_i = jnp.zeros((part, SUB), jnp.float32)
    for l in range(layers):
        weights = weighting[l]
        re = slice(2 * l * part, (2 * l + 1) * part)
        im = slice((2 * l + 1) * part, (2 * l + 2) * part)
        raw_r = raw[re, 0:SUB] - raw[im, SUB:2 * SUB]
        raw_i = raw[re, SUB:2 * SUB] + raw[im, 0:SUB]
        total_r += (raw_r * weights).astype(jnp.bfloat16).astype(jnp.float32)
        total_i += (raw_i * weights).astype(jnp.bfloat16).astype(jnp.float32)
    gridded = jnp.concatenate(
        [
            jnp.concatenate([total_r, total_i], axis=1),
            jnp.concatenate([total_i, -total_r], axis=1),
        ],
        axis=0,
    ).astype(jnp.bfloat16)

    def scatter(turn, inner):
        first = scatter_order(turn // 2) * GROUP + lax.rem(turn, 2) * PAIR
        lo = pl.multiple_of(first * CONTRIB, PAIR * CONTRIB)
        back = lax.dot_general(
            gridded, embed[pl.ds(lo, PAIR * CONTRIB), :], dims, preferred_element_type=jnp.float32
        )
        both = (back * 0.5).astype(jnp.bfloat16)
        for t in range(PAIR):
            send2[first + t] = both[:, t * CONTRIB:(t + 1) * CONTRIB]
        for t in range(PAIR):
            f = first + t

            @pl.when(f != me)
            def _():
                pltpu.make_async_remote_copy(
                    src_ref=send2.at[f], dst_ref=recv2.at[me],
                    send_sem=ssem2, recv_sem=rsem2.at[mine],
                    device_id=(layer, f), device_id_type=MESH,
                ).start()

            @pl.when(f == me)
            def _():
                pltpu.make_async_copy(send2.at[f], recv2.at[me], rsem2.at[mine]).start()

        return inner

    lax.fori_loop(0, 2 * groups, scatter, 0)

    out_scale = (facets * CONTRIB) ** -0.5

    def adjoint(step, last):
        g = adjoint_order(step)
        piece = recv2.at[pl.ds(g * GROUP, GROUP)]
        pltpu.make_async_copy(piece, piece, rsem2.at[g]).wait()
        lo = pl.multiple_of(g * GROUP * 2 * CONTRIB, GROUP * 2 * CONTRIB)
        for k in range(tiles // TILES):
            lhs = []
            for t in range(GROUP):
                both = recv2[g * GROUP + t].astype(jnp.float32)
                br = both[0:part]
                bi = both[part:2 * part]
                turned_r = []
                turned_i = []
                for i in range(TILES):
                    pc = phase_c[g * GROUP + t, k * TILES + i:k * TILES + i + 1, :]
                    ps = phase_s[g * GROUP + t, k * TILES + i:k * TILES + i + 1, :]
                    turned_r.append(br * pc - bi * ps)
                    turned_i.append(br * ps + bi * pc)
                lhs.append(jnp.concatenate(turned_r, axis=0).astype(jnp.bfloat16))
                lhs.append(jnp.concatenate(turned_i, axis=0).astype(jnp.bfloat16))
            rows = slice(k * TILES * part, (k + 1) * TILES * part)
            new = total[rows, :] + jnp.dot(
                jnp.concatenate(lhs, axis=1), fine[pl.ds(lo, GROUP * 2 * CONTRIB), :], preferred_element_type=jnp.float32
            )
            if not last:
                total[rows, :] = new
                continue
            for i in range(TILES):
                xs = slice((k * TILES + i) * CONTRIB, (k * TILES + i + 1) * CONTRIB)
                factor = window_here[:, xs] * out_scale
                out_ref[0, :, xs] = new[i * part:(i + 1) * part, 0:CONTRIB] * factor
                out_ref[1, :, xs] = new[i * part:(i + 1) * part, CONTRIB:2 * CONTRIB] * factor

    def early(step, carry):
        adjoint(step, False)
        return carry

    lax.fori_loop(0, groups - 1, early, 0)
    adjoint(groups - 1, True)

    for ref, sem in (
        (send1.at[pl.ds(0, facets * layers - 1)], ssem1),
        (send2.at[pl.ds(0, facets - 1)], ssem2),
        (counts.at[pl.ds(0, layers - 1)], csem.at[0]),
    ):
        pltpu.make_async_copy(ref, ref, sem).wait()


def shards(slabs, window, density, offsets):
    facets = lax.axis_size("facet")
    layers = lax.axis_size("layer")
    cols = slabs.shape[2]
    width = slabs.shape[3]
    part = cols // layers
    f32, bf16 = jnp.float32, jnp.bfloat16
    summed = pl.pallas_call(
        functools.partial(kernel, layers, facets, cols, width),
        out_shape=jax.ShapeDtypeStruct((2, part, width), f32),
        in_specs=[pl.BlockSpec(memory_space=pltpu.HBM)] * 4,
        out_specs=pl.BlockSpec(memory_space=pltpu.VMEM),
        scratch_shapes=[
            pltpu.VMEM(slabs.shape, bf16),
            pltpu.VMEM((layers, part, SUB), jnp.int32),
            pltpu.VMEM((1, width), f32),
            pltpu.VMEM((1, facets), jnp.int32),
            pltpu.VMEM((2 * layers * part, width), f32),
            pltpu.VMEM((facets, width), f32),
            pltpu.VMEM((facets, width), f32),
            pltpu.VMEM((width, 2 * CONTRIB), bf16),
            pltpu.VMEM((2, GROUP * 2 * layers * part, CHUNK), bf16),
            pltpu.VMEM((GROUP * 2 * layers * part, 2 * CONTRIB), f32),
            pltpu.VMEM((facets * layers, 2 * part, CONTRIB), bf16),
            pltpu.VMEM((facets, layers, 2 * part, CONTRIB), bf16),
            pltpu.VMEM((facets * CONTRIB, 2 * SUB), bf16),
            pltpu.VMEM((CONTRIB, SUB), f32),
            pltpu.VMEM((CONTRIB, SUB), f32),
            pltpu.VMEM((CONTRIB, SUB), f32),
            pltpu.VMEM((CONTRIB, SUB), f32),
            pltpu.VMEM((2 * layers * part, 2 * SUB), f32),
            pltpu.VMEM((facets, 2 * part, CONTRIB), bf16),
            pltpu.VMEM((facets, 2 * part, CONTRIB), bf16),
            pltpu.VMEM((facets, CONTRIB), jnp.int32),
            pltpu.VMEM((facets * 2 * CONTRIB, 2 * CONTRIB), bf16),
            pltpu.VMEM((facets, width // CONTRIB, CONTRIB), f32),
            pltpu.VMEM((facets, width // CONTRIB, CONTRIB), f32),
            pltpu.VMEM((2, TILES * part, GROUP * 2 * CONTRIB), bf16),
            pltpu.VMEM((width // CONTRIB * part, 2 * CONTRIB), f32),
            pltpu.VMEM((layers, part, SUB), f32),
            pltpu.SemaphoreType.DMA,
            pltpu.SemaphoreType.DMA((facets // GROUP,)),
            pltpu.SemaphoreType.DMA,
            pltpu.SemaphoreType.DMA((facets // GROUP,)),
            pltpu.SemaphoreType.DMA((2,)),
            pltpu.SemaphoreType.DMA((3,)),
            pltpu.SemaphoreType.REGULAR((facets // GROUP + 2,)),
        ],
        compiler_params=pltpu.CompilerParams(
            collective_id=0, has_side_effects=True, vmem_limit_bytes=(14 + facets) * 1024 * 1024
        ),
    )(
        *(
            pltpu.with_memory_space_constraint(x, pltpu.HBM)
            for x in (slabs, window[None, :], density, offsets[None, :])
        )
    )
    return summed


def solution(mesh):
    placed = (P("layer", None, None, "facet"), P("facet"), P("layer", None, "facet"), P())
    return jax.shard_map(
        shards, mesh=mesh, in_specs=placed, out_specs=P(None, "layer", "facet"), check_vma=False
    )
```

```python
import functools
import math

import jax
import jax.numpy as jnp
from jax import lax
from jax.experimental import pallas as pl
from jax.experimental.pallas import tpu as pltpu
from jax.sharding import PartitionSpec as P

CONTRIB = 128
SUB = 512
GROUP = 4
CHUNK = 512
ROWS = 256
TILES = 8
PAIR = GROUP // 2
STEP = SUB // CONTRIB

MESH = pl.DeviceIdType.MESH

S, X, Y, D = (0, 0), (1, 0), (0, 1), (1, 1)
END_TURNS = (1, 3, 0, 2)
END_PLAN = (
    ((1, S),),
    ((1, X),),
    ((3, S), (0, S), (0, X), (0, Y), (0, D),),
    ((3, X), (3, Y),),
    ((3, D), (1, Y), (1, D), (2, S), (2, X), (2, Y), (2, D),),
)
INNER_TURNS = (2, 3, 0, 1)
INNER_PLAN = (
    ((2, S),),
    ((3, S), (2, X),),
    ((3, X), (3, Y),),
    ((3, D), (0, S), (0, X), (0, Y), (0, D), (2, Y), (2, D), (1, S), (1, X), (1, Y), (1, D),),
    (),
)


def sincos(turns, period):
    quarter = jnp.floor(turns.astype(jnp.float32) * (4.0 / period) + 0.5).astype(jnp.int32)
    rest = 4 * turns - quarter * period
    y = rest.astype(jnp.float32) * (0.5 * math.pi / period)
    z = y * y
    s = y + y * z * (-1.0 / 6 + z * (1.0 / 120 + z * (-1.0 / 5040 + z * (1.0 / 362880))))
    c = 1.0 + z * (-0.5 + z * (1.0 / 24 + z * (-1.0 / 720 + z * (1.0 / 40320))))
    odd = (quarter & 1) == 1
    cos_abs = jnp.where(odd, s, c)
    sin_abs = jnp.where(odd, c, s)
    cos_part = jnp.where(((quarter + 1) & 2) == 2, -cos_abs, cos_abs)
    sin_part = jnp.where((quarter & 2) == 2, -sin_abs, sin_abs)
    return cos_part, sin_part


def remainder(value, period):
    return value - jnp.floor(value.astype(jnp.float32) * (1.0 / period)).astype(jnp.int32) * period


def kernel(
    layers, facets, cols, width,
    slab_ref, window_ref, density_ref, offset_ref,
    out_ref,
    slab, counts, window_here, offset_here, wind, ca, sa, table, modulated, acc,
    send1, recv1, embed, kr, ki, rr, ri, raw,
    send2, recv2, offs_wide, fine, phase_c, phase_s, turned, total, weighting,
    ssem1, rsem1, ssem2, rsem2, csem, local_sem, reach_sem,
):
    layer = lax.axis_index("layer")
    me = lax.axis_index("facet")
    image = facets * width
    groups = facets // GROUP
    part = cols // layers
    band = layers * part
    mine = me // GROUP
    half = mine // (groups // 2)
    half_groups = groups // 2

    def ranked(step, end, inner):
        mirrored = jnp.where(half == 0, mine, groups - 1 - mine)
        g = jnp.where(mirrored == 0, end[0], inner[0])
        for i in range(1, groups):
            g = jnp.where(step == i, jnp.where(mirrored == 0, end[i], inner[i]), g)
        return jnp.where(half == 0, g, groups - 1 - g)

    def encode_order(step):
        if groups == 4:
            return ranked(step, END_TURNS, INNER_TURNS)
        return outward(step)

    def gather_order(step):
        if groups == 4:
            return ranked(step, (0, 1, 2, 3), (1, 0, 3, 2))
        return inward(step)

    def scatter_order(step):
        if groups == 4:
            return ranked(step, (3, 0, 1, 2), (0, 1, 3, 2))
        return outward(step)

    def adjoint_order(step):
        if groups == 4:
            return ranked(step, (0, 3, 2, 1), (1, 0, 3, 2))
        return inward(step)

    def outward(step):
        return jnp.where(
            half == 0,
            lax.rem(half_groups + step, groups),
            lax.rem(half_groups - 1 - step + groups, groups),
        )

    def inward(step):
        return jnp.where(half == 0, step, groups - 1 - step)

    def signal(sem, where):
        pl.semaphore_signal(sem, inc=1, device_id=where, device_id_type=MESH)

    near = [(layer, me ^ 2)] + [(lax.rem(layer + l, layers), me) for l in range(1, layers)]
    has_up = mine < groups - 1
    has_down = mine > 0

    barrier = pltpu.get_barrier_semaphore()
    signal(barrier, (layer, me ^ 1))
    for core in range(2):
        for there, f in near:
            signal(barrier, (there, f ^ core))

        @pl.when(has_up)
        def _():
            signal(barrier, (layer, (me + GROUP) ^ core))

        @pl.when(has_down)
        def _():
            signal(barrier, (layer, (me - GROUP) ^ core))

    fetch_offsets = pltpu.make_async_copy(offset_ref, offset_here, local_sem.at[2])
    fetch_offsets.start()
    fetch_window = pltpu.make_async_copy(window_ref, window_here, local_sem.at[1])
    fetch_window.start()
    fetch_slab = pltpu.make_async_copy(slab_ref, slab, local_sem.at[0])
    fetch_slab.start()

    def tell(reach):
        for where in near:
            signal(reach_sem.at[reach], where)

        @pl.when(has_up)
        def _():
            signal(reach_sem.at[reach], (layer, me + GROUP))

        @pl.when(has_down)
        def _():
            signal(reach_sem.at[reach], (layer, me - GROUP))

    def meet(reach):
        @pl.when(jnp.logical_and(has_up, has_down))
        def _():
            pl.semaphore_wait(reach_sem.at[reach], len(near) + 2)

        @pl.when(jnp.logical_not(jnp.logical_and(has_up, has_down)))
        def _():
            pl.semaphore_wait(reach_sem.at[reach], len(near) + 1)

    def spread_rows(count, stride):
        lane = lax.broadcasted_iota(jnp.int32, (count, CONTRIB), 1) * STEP
        row = lax.broadcasted_iota(jnp.int32, (count, CONTRIB), 0) * stride
        return lane, remainder(lane * row, image)

    lane, turns = spread_rows(8, 1)
    low_c, low_s = sincos(remainder(lane * me, facets) * width + turns, image)
    mid_c, mid_s = sincos(spread_rows(ROWS // 8, 8)[1], image)
    high_c, high_s = sincos(spread_rows(-(-width // ROWS // 8) * 8, ROWS)[1], image)
    base_c = jnp.concatenate(
        [low_c * mid_c[i:i + 1] - low_s * mid_s[i:i + 1] for i in range(ROWS // 8)], axis=0
    )
    base_s = jnp.concatenate(
        [low_c * mid_s[i:i + 1] + low_s * mid_c[i:i + 1] for i in range(ROWS // 8)], axis=0
    )
    for k in range(width // ROWS):
        rot_c = high_c[k:k + 1]
        rot_s = high_s[k:k + 1]
        table[k * ROWS:(k + 1) * ROWS, 0:CONTRIB] = (base_c * rot_c - base_s * rot_s).astype(jnp.bfloat16)
        table[k * ROWS:(k + 1) * ROWS, CONTRIB:2 * CONTRIB] = (
            base_c * rot_s + base_s * rot_c
        ).astype(jnp.bfloat16)

    fetch_offsets.wait()
    square = (GROUP * groups, GROUP * groups)
    on_diagonal = lax.broadcasted_iota(jnp.int32, square, 0) == lax.broadcasted_iota(jnp.int32, square, 1)
    offs = jnp.sum(
        jnp.where(on_diagonal, offset_here[...].astype(jnp.float32), 0.0), axis=1, keepdims=True
    ).astype(jnp.int32)
    offs_wide[...] = jnp.broadcast_to(offs, offs_wide.shape)
    cell = lax.broadcasted_iota(jnp.int32, (facets, CONTRIB), 1)
    tile = jnp.minimum(cell, width // CONTRIB - 1) * CONTRIB
    within_c, within_s = sincos(remainder(offs * cell, image), image)
    tile_c, tile_s = sincos(
        remainder(offs * me, facets) * width + remainder(offs * tile, image), image
    )
    for k in range(width // CONTRIB):
        at_c = tile_c[:, k:k + 1]
        at_s = tile_s[:, k:k + 1]
        xs = slice(k * CONTRIB, (k + 1) * CONTRIB)
        ca[:, xs] = within_c * at_c - within_s * at_s
        sa[:, xs] = within_c * at_s + within_s * at_c

    fetch_window.wait()
    fetch_slab.wait()
    window = window_here[...]
    for p in range(2):
        whole = (slab[0, p].astype(jnp.float32) * window).astype(jnp.bfloat16).astype(jnp.float32)
        wind[p * band:(p + 1) * band, :] = whole

    scale1 = width ** -0.5

    def deliver(h, s):
        pltpu.make_async_remote_copy(
            src_ref=send1.at[s * layers + h], dst_ref=recv1.at[me, layer],
            send_sem=ssem1, recv_sem=rsem1.at[mine],
            device_id=(h, s), device_id_type=MESH,
        ).start()

    def planned(turn):
        outer = jnp.logical_or(mine == 0, mine == groups - 1)
        for i in range(groups + 1):
            for at_end, plan in ((True, END_PLAN[i]), (False, INNER_PLAN[i])):
                if not plan:
                    continue

                @pl.when(jnp.logical_and(turn == i, outer if at_end else jnp.logical_not(outer)))
                def _():
                    for g, (dx, dl) in plan:
                        there = jnp.where(half == 0, g, groups - 1 - g)
                        straight = there * GROUP + lax.rem(me, GROUP)
                        home = g == (0 if at_end else 1) and not dx and not dl
                        for core in range(2):
                            if home and core == 0:
                                pltpu.make_async_copy(
                                    send1.at[me * layers + layer], recv1.at[me, layer], rsem1.at[mine]
                                ).start()
                            else:
                                deliver(layer ^ dl, straight ^ (2 * dx + core))

    def dispatch(turn):
        if groups == 4 and layers == 2:
            planned(turn)
            return

        def slot(a, carry):
            g = encode_order(a)
            ahead = jnp.abs(g - mine)
            straight = g * GROUP + lax.rem(me, GROUP)
            for off in range(3):
                reach = ahead + off
                late = jnp.logical_and(a < turn, reach == turn + 1)
                fresh = jnp.logical_and(a == turn, reach <= turn + 1)

                @pl.when(jnp.logical_or(late, fresh))
                def _():
                    if off == 0:
                        deliver(layer, straight ^ 1)

                        @pl.when(g != mine)
                        def _():
                            deliver(layer, straight)

                        @pl.when(g == mine)
                        def _():
                            pltpu.make_async_copy(
                                send1.at[me * layers + layer], recv1.at[me, layer], rsem1.at[mine]
                            ).start()

                    for core in range(2):
                        if off == 1:
                            deliver(layer, straight ^ (2 + core))
                        if off > 0:
                            for l in range(1, layers):
                                deliver(lax.rem(layer + l, layers), straight ^ (2 * off - 2 + core))

            return carry

        lax.fori_loop(0, groups, slot, 0)

    def encode(turn, carry):
        step = turn
        g = encode_order(step)
        for k in range(width // CHUNK):
            xs = slice(k * CHUNK, (k + 1) * CHUNK)
            rows = []
            for t in range(GROUP):
                s = g * GROUP + t
                c_row = ca[pl.ds(s, 1), xs]
                s_row = sa[pl.ds(s, 1), xs]
                wr = wind[0:band, xs]
                wi = wind[band:2 * band, xs]
                rows.append((wr * c_row + wi * s_row).astype(jnp.bfloat16))
                rows.append((wi * c_row - wr * s_row).astype(jnp.bfloat16))
            prod = jnp.dot(
                jnp.concatenate(rows, axis=0), table[xs, :], preferred_element_type=jnp.float32
            )
            if k == 0:
                acc[...] = prod
            else:
                acc[...] += prod
        for t in range(GROUP):
            lo = t * 2 * band
            pr = acc[lo:lo + band, :]
            pi = acc[lo + band:lo + 2 * band, :]
            real = (pr[:, :CONTRIB] + pi[:, CONTRIB:]) * scale1
            imag = (pi[:, :CONTRIB] - pr[:, CONTRIB:]) * scale1
            for h in range(layers):
                hs = slice(h * part, (h + 1) * part)
                send1[(g * GROUP + t) * layers + h] = jnp.concatenate([real[hs], imag[hs]], axis=0).astype(jnp.bfloat16)

        @pl.when(turn == 0)
        def _():
            both = jnp.logical_and(has_up, has_down)

            @pl.when(both)
            def _():
                pl.semaphore_wait(barrier, 1 + 2 * (len(near) + 2))

            @pl.when(jnp.logical_not(both))
            def _():
                pl.semaphore_wait(barrier, 1 + 2 * (len(near) + 1))

            tell(2)

        @pl.when(turn > 0)
        def _():
            meet(turn + 1)
            tell(turn + 2)

        dispatch(turn)

        @pl.when(turn == 0)
        def _():
            for l in range(layers):

                @pl.when(layer == l)
                def _():
                    pltpu.make_async_copy(
                        density_ref.at[0, l * part:(l + 1) * part], counts.at[l], csem.at[1]
                    ).start()

                @pl.when(layer != l)
                def _():
                    pltpu.make_async_remote_copy(
                        src_ref=density_ref.at[0, l * part:(l + 1) * part], dst_ref=counts.at[layer],
                        send_sem=csem.at[0], recv_sem=csem.at[1],
                        device_id=(l, me), device_id_type=MESH,
                    ).start()

        return carry

    lax.fori_loop(0, groups, encode, 0)
    meet(groups + 1)
    dispatch(groups)

    spacing = lax.broadcasted_iota(jnp.int32, (CONTRIB, SUB), 1) - STEP * lax.broadcasted_iota(
        jnp.int32, (CONTRIB, SUB), 0
    )
    scaled = spacing.astype(jnp.float32) * (1.0 / STEP)
    weight_k = 1.0 / (1.0 + scaled * scaled)
    c0, s0 = sincos(spacing, 2 * facets)
    kr[...] = c0 * weight_k
    ki[...] = s0 * weight_k
    c1, s1 = sincos(spacing, facets)
    rr[...] = c1
    ri[...] = s1

    def make_embed(f, carry):
        r = kr[...]
        i = ki[...]
        lo = pl.multiple_of(f * CONTRIB, CONTRIB)
        embed[pl.ds(lo, CONTRIB), 0:SUB] = r.astype(jnp.bfloat16)
        embed[pl.ds(lo, CONTRIB), SUB:2 * SUB] = (-i).astype(jnp.bfloat16)
        a = rr[...]
        b = ri[...]
        kr[...] = r * a - i * b
        ki[...] = r * b + i * a
        return carry

    lax.fori_loop(0, facets, make_embed, 0)

    tiles = width // CONTRIB
    square = (CONTRIB, CONTRIB)
    lane_here = lax.broadcasted_iota(jnp.int32, square, 1)
    fine_c, fine_s = sincos(
        remainder(STEP * lax.broadcasted_iota(jnp.int32, square, 0) * lane_here, image), image
    )
    kr[:, 0:CONTRIB] = fine_c
    ki[:, 0:CONTRIB] = fine_s
    coarse = CONTRIB * lax.broadcasted_iota(jnp.int32, (tiles, CONTRIB), 0)
    steps = STEP * lax.broadcasted_iota(jnp.int32, (tiles, CONTRIB), 1)

    def make_phases(f, carry):
        off = offs_wide[pl.ds(f, 1), :]
        c, i = sincos(remainder(off * lane_here[0:1], image), image)
        fc = kr[:, 0:CONTRIB] * c - ki[:, 0:CONTRIB] * i
        fs = kr[:, 0:CONTRIB] * i + ki[:, 0:CONTRIB] * c
        lo = pl.multiple_of(f * 2 * CONTRIB, 2 * CONTRIB)
        fine[pl.ds(lo, CONTRIB), 0:CONTRIB] = fc.astype(jnp.bfloat16)
        fine[pl.ds(lo, CONTRIB), CONTRIB:2 * CONTRIB] = fs.astype(jnp.bfloat16)
        fine[pl.ds(lo + CONTRIB, CONTRIB), 0:CONTRIB] = (-fs).astype(jnp.bfloat16)
        fine[pl.ds(lo + CONTRIB, CONTRIB), CONTRIB:2 * CONTRIB] = fc.astype(jnp.bfloat16)
        frequency = off + steps
        pc, ps = sincos(
            remainder(frequency * me, facets) * width + remainder(frequency * coarse, image), image
        )
        phase_c[f] = pc
        phase_s[f] = ps
        return carry

    lax.fori_loop(0, facets, make_phases, 0)
    total[...] = jnp.zeros_like(total)

    pltpu.make_async_copy(counts, counts, csem.at[1]).wait()
    sub_scale = (2 * facets) ** -0.5
    dims = (((1,), (1,)), ((), ()))

    for l in range(layers):
        here = counts[l]
        weighting[l] = jnp.where(
            here > 0, 1.0 / jnp.maximum(here, 1).astype(jnp.float32), 0.0
        ) * sub_scale
    raw[...] = jnp.zeros_like(raw)

    def gather(step, inner):
        g = gather_order(step)
        piece = recv1.at[pl.ds(g * GROUP, GROUP)]
        pltpu.make_async_copy(piece, piece, rsem1.at[g]).wait()
        lhs = jnp.concatenate(
            [recv1[g * GROUP + t].reshape(2 * band, CONTRIB) for t in range(GROUP)], axis=1
        )
        lo = pl.multiple_of(g * GROUP * CONTRIB, GROUP * CONTRIB)
        raw[...] += jnp.dot(
            lhs, embed[pl.ds(lo, GROUP * CONTRIB), :], preferred_element_type=jnp.float32
        )
        return inner

    lax.fori_loop(0, groups, gather, 0)

    total_r = jnp.zeros((part, SUB), jnp.float32)
    total_i = jnp.zeros((part, SUB), jnp.float32)
    for l in range(layers):
        weights = weighting[l]
        re = slice(2 * l * part, (2 * l + 1) * part)
        im = slice((2 * l + 1) * part, (2 * l + 2) * part)
        raw_r = raw[re, 0:SUB] - raw[im, SUB:2 * SUB]
        raw_i = raw[re, SUB:2 * SUB] + raw[im, 0:SUB]
        total_r += (raw_r * weights).astype(jnp.bfloat16).astype(jnp.float32)
        total_i += (raw_i * weights).astype(jnp.bfloat16).astype(jnp.float32)
    gridded = jnp.concatenate(
        [
            jnp.concatenate([total_r, total_i], axis=1),
            jnp.concatenate([total_i, -total_r], axis=1),
        ],
        axis=0,
    ).astype(jnp.bfloat16)

    def scatter(turn, inner):
        first = scatter_order(turn // 2) * GROUP + lax.rem(turn, 2) * PAIR
        lo = pl.multiple_of(first * CONTRIB, PAIR * CONTRIB)
        back = lax.dot_general(
            gridded, embed[pl.ds(lo, PAIR * CONTRIB), :], dims, preferred_element_type=jnp.float32
        )
        both = (back * 0.5).astype(jnp.bfloat16)
        for t in range(PAIR):
            send2[first + t] = both[:, t * CONTRIB:(t + 1) * CONTRIB]
        for t in range(PAIR):
            f = first + t

            @pl.when(f != me)
            def _():
                pltpu.make_async_remote_copy(
                    src_ref=send2.at[f], dst_ref=recv2.at[me],
                    send_sem=ssem2, recv_sem=rsem2.at[mine],
                    device_id=(layer, f), device_id_type=MESH,
                ).start()

            @pl.when(f == me)
            def _():
                pltpu.make_async_copy(send2.at[f], recv2.at[me], rsem2.at[mine]).start()

        return inner

    lax.fori_loop(0, 2 * groups, scatter, 0)

    out_scale = (facets * CONTRIB) ** -0.5

    def adjoint(step, last):
        g = adjoint_order(step)
        piece = recv2.at[pl.ds(g * GROUP, GROUP)]
        pltpu.make_async_copy(piece, piece, rsem2.at[g]).wait()
        lo = pl.multiple_of(g * GROUP * 2 * CONTRIB, GROUP * 2 * CONTRIB)
        for k in range(tiles // TILES):
            lhs = []
            for t in range(GROUP):
                both = recv2[g * GROUP + t].astype(jnp.float32)
                br = both[0:part]
                bi = both[part:2 * part]
                turned_r = []
                turned_i = []
                for i in range(TILES):
                    pc = phase_c[g * GROUP + t, k * TILES + i:k * TILES + i + 1, :]
                    ps = phase_s[g * GROUP + t, k * TILES + i:k * TILES + i + 1, :]
                    turned_r.append(br * pc - bi * ps)
                    turned_i.append(br * ps + bi * pc)
                lhs.append(jnp.concatenate(turned_r, axis=0).astype(jnp.bfloat16))
                lhs.append(jnp.concatenate(turned_i, axis=0).astype(jnp.bfloat16))
            rows = slice(k * TILES * part, (k + 1) * TILES * part)
            new = total[rows, :] + jnp.dot(
                jnp.concatenate(lhs, axis=1), fine[pl.ds(lo, GROUP * 2 * CONTRIB), :], preferred_element_type=jnp.float32
            )
            if not last:
                total[rows, :] = new
                continue
            for i in range(TILES):
                xs = slice((k * TILES + i) * CONTRIB, (k * TILES + i + 1) * CONTRIB)
                factor = window_here[:, xs] * out_scale
                out_ref[0, :, xs] = new[i * part:(i + 1) * part, 0:CONTRIB] * factor
                out_ref[1, :, xs] = new[i * part:(i + 1) * part, CONTRIB:2 * CONTRIB] * factor

    def early(step, carry):
        adjoint(step, False)
        return carry

    lax.fori_loop(0, groups - 1, early, 0)
    adjoint(groups - 1, True)

    for ref, sem in (
        (send1.at[pl.ds(0, facets * layers - 1)], ssem1),
        (send2.at[pl.ds(0, facets - 1)], ssem2),
        (counts.at[pl.ds(0, layers - 1)], csem.at[0]),
    ):
        pltpu.make_async_copy(ref, ref, sem).wait()


def shards(slabs, window, density, offsets):
    facets = lax.axis_size("facet")
    layers = lax.axis_size("layer")
    cols = slabs.shape[2]
    width = slabs.shape[3]
    part = cols // layers
    f32, bf16 = jnp.float32, jnp.bfloat16
    summed = pl.pallas_call(
        functools.partial(kernel, layers, facets, cols, width),
        out_shape=jax.ShapeDtypeStruct((2, part, width), f32),
        in_specs=[pl.BlockSpec(memory_space=pltpu.HBM)] * 4,
        out_specs=pl.BlockSpec(memory_space=pltpu.VMEM),
        scratch_shapes=[
            pltpu.VMEM(slabs.shape, bf16),
            pltpu.VMEM((layers, part, SUB), jnp.int32),
            pltpu.VMEM((1, width), f32),
            pltpu.VMEM((1, facets), jnp.int32),
            pltpu.VMEM((2 * layers * part, width), f32),
            pltpu.VMEM((facets, width), f32),
            pltpu.VMEM((facets, width), f32),
            pltpu.VMEM((width, 2 * CONTRIB), bf16),
            pltpu.VMEM((2, GROUP * 2 * layers * part, CHUNK), bf16),
            pltpu.VMEM((GROUP * 2 * layers * part, 2 * CONTRIB), f32),
            pltpu.VMEM((facets * layers, 2 * part, CONTRIB), bf16),
            pltpu.VMEM((facets, layers, 2 * part, CONTRIB), bf16),
            pltpu.VMEM((facets * CONTRIB, 2 * SUB), bf16),
            pltpu.VMEM((CONTRIB, SUB), f32),
            pltpu.VMEM((CONTRIB, SUB), f32),
            pltpu.VMEM((CONTRIB, SUB), f32),
            pltpu.VMEM((CONTRIB, SUB), f32),
            pltpu.VMEM((2 * layers * part, 2 * SUB), f32),
            pltpu.VMEM((facets, 2 * part, CONTRIB), bf16),
            pltpu.VMEM((facets, 2 * part, CONTRIB), bf16),
            pltpu.VMEM((facets, CONTRIB), jnp.int32),
            pltpu.VMEM((facets * 2 * CONTRIB, 2 * CONTRIB), bf16),
            pltpu.VMEM((facets, width // CONTRIB, CONTRIB), f32),
            pltpu.VMEM((facets, width // CONTRIB, CONTRIB), f32),
            pltpu.VMEM((2, TILES * part, GROUP * 2 * CONTRIB), bf16),
            pltpu.VMEM((width // CONTRIB * part, 2 * CONTRIB), f32),
            pltpu.VMEM((layers, part, SUB), f32),
            pltpu.SemaphoreType.DMA,
            pltpu.SemaphoreType.DMA((facets // GROUP,)),
            pltpu.SemaphoreType.DMA,
            pltpu.SemaphoreType.DMA((facets // GROUP,)),
            pltpu.SemaphoreType.DMA((2,)),
            pltpu.SemaphoreType.DMA((3,)),
            pltpu.SemaphoreType.REGULAR((facets // GROUP + 2,)),
        ],
        compiler_params=pltpu.CompilerParams(
            collective_id=0, has_side_effects=True, vmem_limit_bytes=(14 + facets) * 1024 * 1024
        ),
    )(
        *(
            pltpu.with_memory_space_constraint(x, pltpu.HBM)
            for x in (slabs, window[None, :], density, offsets[None, :])
        )
    )
    return summed


def solution(mesh):
    placed = (P("layer", None, None, "facet"), P("facet"), P("layer", None, "facet"), P())
    return jax.shard_map(
        shards, mesh=mesh, in_specs=placed, out_specs=P(None, "layer", "facet"), check_vma=False
    )
```
